256 devices in a mesh: row: 32 (over x_hi, z, core), col: 8 (over x_lo, y).
Axes of the slice: x: 4 (x_hi: 2, x_lo: 2; x = x_hi * 2 + x_lo), y: 4, z: 8, core: 2. Of those that a mesh axis runs over, the one named last changes fastest.
Arguments:
- eigvecs: float32 [8192, 8192], P('row', 'col'), may hold values from -6 to 6
- panels: float32 [5, 32, 256, 128], P(None, 'row', 'col'), may hold values from -6 to 6
- sweep_shift: int32 [5], replicated, may hold values from 0 to 31
- slot_group: int32 [5, 32], replicated, may hold values from 0 to 31, each once within a row
Outputs:
- full_vectors: float32 [8192, 8192], P('row', 'col')
The draws below stay inside these ranges and needn't reach their ends.
Inputs may be any that keep to these rules, and one draw needn't show every extreme that they name: Each row of slot_group names each of the 32 groups once.
All inputs are finite; a program needn't handle non-finite values.
Results may differ from the reference program's by a relative error of at most 0.00029.
Values sent between devices are 32-bit elements; how exact they have to be, the bound alone decides.
A program may use at most 128 MiB of HBM per device.

```python
import jax
import jax.numpy as jnp
from jax import lax

B = 128
SWEEPS = 5
W = 256
NROWS = 8192
NCOLS = 8192
NG = 32


def set_ends(drawn, own_key, least, top_value):
    dims = drawn.shape
    index_at = [jax.random.randint(jax.random.fold_in(own_key, axis), (), 0, dims[axis]) for axis in range(len(dims))]
    drawn = drawn.at[tuple(index_at)].set(least)
    longest = dims.index(max(dims))
    index_at[longest] = (index_at[longest] + 1) % dims[longest]
    return drawn.at[tuple(index_at)].set(top_value)


def block_levels(key, shape, pieces, smallest, largest):
    gain, own = 1.0, jax.random.fold_in(key, 6)
    for position, shards_of in pieces:
        draws = jnp.exp(jax.random.uniform(jax.random.fold_in(own, position), (shards_of,), jnp.float32, smallest / len(pieces), largest / len(pieces)))
        gain = gain * jnp.repeat(draws, shape[position] // shards_of).reshape([-1 if axis == position else 1 for axis in range(len(shape))])
    return gain


def noise(key, shape, width, most, shards=(), held_as=jnp.bfloat16):
    drawn = width * jax.random.normal(key, shape, jnp.float32)
    if shards:
        drawn = drawn * block_levels(key, shape, shards, -0.22, 0.18)
    return jnp.clip(drawn, -most, most).astype(held_as)


def setup_inputs(seed: int = 0) -> dict:
    splits = jax.random.split(jax.random.key(seed), 5)
    return {
        "eigvecs": noise(splits[0], (NROWS, NCOLS), 1.0, 6.0, ((0, 32), (1, 8)), jnp.float32),
        "panels": noise(splits[1], (SWEEPS, NG, W, B), 1.0, 6.0, ((1, 32), (2, 8)), jnp.float32),
        "sweep_shift": set_ends(jax.random.randint(splits[2], (SWEEPS,), 0, NG), jax.random.fold_in(splits[2], 1), 0, NG - 1).astype(jnp.int32),
        "slot_group": jax.vmap(lambda own: jax.random.permutation(own, NG))(jax.random.split(splits[3], SWEEPS)).reshape((SWEEPS, NG)).astype(jnp.int32),
    }


PRECISE = lax.Precision.HIGHEST

def apply_groups(vectors, windows):
    products = jnp.einsum('gwb,gwc->gbc', vectors, vectors, precision=PRECISE)
    ident = jnp.eye(products.shape[1], dtype=products.dtype)
    factor = jnp.triu(products, 1) + 0.5 * products * ident
    projected = jnp.einsum('gwb,gwc->gbc', vectors, windows, precision=PRECISE)
    coeffs = lax.linalg.triangular_solve(factor, projected, left_side=True, lower=False)
    return windows - jnp.einsum('gwb,gbc->gwc', vectors, coeffs, precision=PRECISE)

def reference(eigvecs, panels, sweep_shift, slot_group):
    all_rows = eigvecs.shape[0]
    all_cols = eigvecs.shape[1]
    positions = jnp.arange(NG, dtype=jnp.int32)
    for sweep_step in range(SWEEPS):
        leading = sweep_step % 2 * B
        rolled = jnp.roll(eigvecs, -leading, axis=0)
        windows = rolled.reshape(NG, 2 * B, all_cols)
        wanted = (positions - sweep_shift[sweep_step]) % NG
        holder = jnp.argsort(slot_group[sweep_step]).astype(jnp.int32)
        slots = holder[wanted.astype(jnp.int32)]
        vectors = panels[sweep_step][slots]
        windows = apply_groups(vectors, windows)
        eigvecs = jnp.roll(windows.reshape(all_rows, all_cols), leading, axis=0)
    return eigvecs
```

```python
import functools

import jax
import jax.numpy as jnp
from jax import lax
from jax.experimental import pallas as pl
from jax.experimental.pallas import tpu as pltpu
from jax.sharding import PartitionSpec as P

MESH = pl.DeviceIdType.MESH
F32, BF16 = jnp.float32, jnp.bfloat16
B = 128
SWEEPS = 5
ROWS, COLS = 32, 8
RING = 8
PIECE = 32
GROUPS = ((0, 1), (1, 3), (3, 5))
WINDOWS = ((0, 0), (1, 0), (1, 1), (2, 0), (3, 0), (3, 1), (4, 0))
CHUNK = 256
CHUNKS = 1024 // CHUNK


def copy_ids():
    ids = {}
    for g in range(len(GROUPS)):
        names = [("across", g)]
        names += [("up", g, 1, item) for item in (0, 1)] + [("down", g, 1, item) for item in (0, 1)]
        names += [("up", g, t) for t in (2, 3, 4)] + [("down", g, t) for t in (2, 3)]
        names += [("mate", g, "own", item) for item in (0, 1)]
        names += [("mate", g, "up", t) for t in (1, 2, 3, 4)] + [("mate", g, "down", t) for t in (1, 2, 3)]
        for name in names:
            ids[name] = len(ids)
    for w in range(len(WINDOWS)):
        for j in range(1, COLS):
            ids[("col", w, j)] = len(ids)
    for x in (0, 1):
        for side in ("prev", "next"):
            for j in range(CHUNKS):
                ids[(side, x, j)] = len(ids)
    return ids


IDS = copy_ids()


def split(a):
    high = a.astype(BF16)
    return high, (a - high.astype(F32)).astype(BF16)


def dot3(a, b, dims=((1,), (0,))):
    (ah, al), (bh, bl) = a, b
    dot = lambda x, y: lax.dot_general(x, y, (dims, ((), ())), preferred_element_type=F32)
    return dot(ah, bh) + (dot(ah, bl) + dot(al, bh))


def dot6(a, b, dims=((1,), (0,))):
    return lax.dot_general(a, b, (dims, ((), ())), precision=lax.Precision.HIGHEST, preferred_element_type=F32)


def inverse(products):
    row = lax.broadcasted_iota(jnp.int32, (B, B), 0)
    col = lax.broadcasted_iota(jnp.int32, (B, B), 1)
    diagonal = jnp.where(row == col, products, 0.0)
    down = 2.0 / jnp.sum(diagonal, axis=1, keepdims=True)
    along = 2.0 / jnp.sum(diagonal, axis=0, keepdims=True)
    first = (col == row + 1) & ((row & 1) == 0)
    inv = jnp.where(row == col, down, 0.0) - jnp.where(first, down * products * along, 0.0)
    width = 2
    while width < B:
        pair = 2 * width
        corner = ((row & -pair) == (col & -pair)) & ((row & width) == 0) & ((col & width) != 0)
        off = jnp.where(corner, products, 0.0)
        inv = inv - dot6(dot6(inv, off), inv)
        width = pair
    return inv


def reflector(panel_ref):
    panel = panel_ref[...]
    inv = inverse(dot6(panel, panel, ((0,), (0,))))
    v = split(panel)
    return v, dot3(v, split(inv))


def transform(v, vt, top):
    rows = slice(0, B) if top else slice(B, 2 * B)
    row = lax.broadcasted_iota(jnp.int32, (B, 2 * B), 0) + (0 if top else B)
    col = lax.broadcasted_iota(jnp.int32, (B, 2 * B), 1)
    ident = jnp.where(row == col, 1.0, 0.0)
    return split(ident - dot3(split(vt[rows]), v, ((1,), (1,))))


def kernel(
    z_ref, panels, shift, slots, out_ref,
    gathered, stage, full, first, second, from_prev, from_next, hh, hl, send_sem, recv_sem,
):
    r, c = lax.axis_index("row"), lax.axis_index("col")
    k = lax.rem(r, 2)
    z = lax.rem(lax.div(r, 2), RING)
    h = lax.div(r, 2 * RING)
    row_of = lambda h_, z_, k_: (h_ * RING + z_) * 2 + k_
    ring = lambda d: lax.rem(z + d + RING, RING)
    up, down = row_of(h, ring(1), k), row_of(h, ring(-1), k)
    mate, across = row_of(h, z, 1 - k), row_of(1 - h, z, k)
    prev_row, next_row = lax.rem(r + ROWS - 1, ROWS), lax.rem(r + 1, ROWS)
    other_col = lambda j: lax.rem(c + j + COLS, COLS)
    sent = []

    def send(name, src, dst, row, col):
        i = IDS[name]
        copy = pltpu.make_async_remote_copy(
            src_ref=src, dst_ref=dst, send_sem=send_sem.at[i], recv_sem=recv_sem.at[i],
            device_id=(row, col), device_id_type=MESH,
        )
        copy.start()
        sent.append(copy)

    def arrive(name, dst):
        i = IDS[name]
        pltpu.make_async_remote_copy(
            src_ref=dst, dst_ref=dst, send_sem=send_sem.at[i], recv_sem=recv_sem.at[i],
            device_id=(mate, c), device_id_type=MESH,
        ).wait_recv()

    barrier = pltpu.get_barrier_semaphore()
    partners = [(up, c), (down, c), (mate, c), (across, c), (prev_row, c), (next_row, c)]
    partners += [(r, other_col(j)) for j in range(1, COLS)]
    for partner in partners:
        pl.semaphore_signal(barrier, inc=1, device_id=partner, device_id_type=MESH)
    pl.semaphore_wait(barrier, len(partners))

    spans = [pl.ds(a, b - a) for a, b in GROUPS]
    for g, span in enumerate(spans):
        own = gathered.at[span, k, z, h]
        send(("across", g), panels.at[span], own, across, c)
        send(("up", g, 1, 0), panels.at[span], own, up, c)
        send(("down", g, 1, 0), panels.at[span], own, down, c)
        send(("mate", g, "own", 0), panels.at[span], own, mate, c)
    for s in range(SWEEPS):
        gathered[s, k, z, h] = panels[s]
    for g, span in enumerate(spans):
        other = gathered.at[span, k, z, 1 - h]
        arrive(("across", g), other)
        send(("up", g, 1, 1), other, other, up, c)
        send(("down", g, 1, 1), other, other, down, c)
        send(("mate", g, "own", 1), other, other, mate, c)
    for t in (1, 2, 3, 4):
        for g, span in enumerate(spans):
            for side, sign, steps, onward in (("up", -1, 4, up), ("down", 1, 3, down)):
                if t > steps:
                    continue
                at = ring(sign * t)
                block = gathered.at[span, k, at]
                if t == 1:
                    arrive((side, g, 1, 0), gathered.at[span, k, at, h])
                    arrive((side, g, 1, 1), gathered.at[span, k, at, 1 - h])
                else:
                    arrive((side, g, t), block)
                if t < steps:
                    send((side, g, t + 1), block, block, onward, c)
                send(("mate", g, side, t), block, block, mate, c)
    for g, span in enumerate(spans):
        arrive(("mate", g, "own", 0), gathered.at[span, 1 - k, z, h])
        arrive(("mate", g, "own", 1), gathered.at[span, 1 - k, z, 1 - h])
        for side, sign, steps in (("up", -1, 4), ("down", 1, 3)):
            for t in range(1, steps + 1):
                arrive(("mate", g, side, t), gathered.at[span, 1 - k, ring(sign * t)])

    for w, (s, back) in enumerate(WINDOWS):
        wanted = lax.rem(r + 2 * ROWS - back - shift[s], ROWS)
        slot = jnp.int32(0)
        for p in range(ROWS):
            slot = jnp.where(slots[s, p] == wanted, p, slot)
        piece = gathered[s, lax.rem(slot, 2), lax.rem(lax.div(slot, 2), RING), lax.div(slot, 2 * RING)]
        stage[w] = piece
        full[w, pl.ds(pl.multiple_of(c * PIECE, PIECE), PIECE)] = piece
    for w in range(len(WINDOWS)):
        place = full.at[w, pl.ds(pl.multiple_of(c * PIECE, PIECE), PIECE)]
        for j in range(1, COLS):
            send(("col", w, j), stage.at[w], place, r, other_col(j))

    def wait_panel(w):
        for j in range(1, COLS):
            arrive(("col", w, j), full.at[w, pl.ds(pl.multiple_of(other_col(-j) * PIECE, PIECE), PIECE)])

    def make_transform(s):
        found = [w for w, (of, _) in enumerate(WINDOWS) if of == s]
        for w in found:
            wait_panel(w)
        for half in (0, 1):
            w = found[0] if half == 0 else found[-1]
            if half == 0 or len(found) == 2:
                v, vt = reflector(full.at[w])
            hh[s, half], hl[s, half] = transform(v, vt, half == 0)

    def times(s, half, top, bottom):
        a = (hh[s, half, :, :B], hl[s, half, :, :B])
        b = (hh[s, half, :, B:], hl[s, half, :, B:])
        return dot3(a, split(top)) + dot3(b, split(bottom))

    def exchange(x, j, block):
        send(("prev", x, j), block.at[j, pl.ds(0, B)], from_next.at[x, j], prev_row, c)
        send(("next", x, j), block.at[j, pl.ds(B, B)], from_prev.at[x, j], next_row, c)

    def odd_even(x, j, block):
        s = 2 * x + 1
        arrive(("prev", x, j), from_next.at[x, j])
        arrive(("next", x, j), from_prev.at[x, j])
        high = times(s, 0, block[j, B:], from_next[x, j])
        low = times(s, 1, from_prev[x, j], block[j, :B])
        return times(s + 1, 0, low, high), times(s + 1, 1, low, high)

    make_transform(0)
    for j in range(CHUNKS):
        cols = slice(j * CHUNK, (j + 1) * CHUNK)
        for half in (0, 1):
            first[j, half * B : half * B + B] = times(0, half, z_ref[:B, cols], z_ref[B:, cols])
        if j:
            exchange(0, j - 1, first)
    make_transform(1)
    exchange(0, CHUNKS - 1, first)
    make_transform(2)
    for j in range(CHUNKS):
        second[j, :B], second[j, B:] = odd_even(0, j, first)
        if j:
            exchange(1, j - 1, second)
    make_transform(3)
    exchange(1, CHUNKS - 1, second)
    make_transform(4)
    for j in range(CHUNKS):
        cols = slice(j * CHUNK, (j + 1) * CHUNK)
        out_ref[:B, cols], out_ref[B:, cols] = odd_even(1, j, second)
    for copy in sent:
        copy.wait_send()


def on_device(eigvecs, panels, sweep_shift, slot_group):
    rows, cols = eigvecs.shape
    vmem, smem = pl.BlockSpec(memory_space=pltpu.VMEM), pl.BlockSpec(memory_space=pltpu.SMEM)
    return pl.pallas_call(
        kernel,
        out_shape=jax.ShapeDtypeStruct((rows, cols), F32),
        in_specs=[vmem, vmem, smem, smem],
        out_specs=vmem,
        scratch_shapes=[
            pltpu.VMEM((SWEEPS, 2, RING, 2, PIECE, B), F32),
            pltpu.VMEM((len(WINDOWS), PIECE, B), F32),
            pltpu.VMEM((len(WINDOWS), 2 * B, B), F32),
            pltpu.VMEM((CHUNKS, 2 * B, CHUNK), F32),
            pltpu.VMEM((CHUNKS, 2 * B, CHUNK), F32),
            pltpu.VMEM((2, CHUNKS, B, CHUNK), F32),
            pltpu.VMEM((2, CHUNKS, B, CHUNK), F32),
            pltpu.VMEM((SWEEPS, 2, B, 2 * B), BF16),
            pltpu.VMEM((SWEEPS, 2, B, 2 * B), BF16),
            pltpu.SemaphoreType.DMA((len(IDS),)),
            pltpu.SemaphoreType.DMA((len(IDS),)),
        ],
        compiler_params=pltpu.CompilerParams(collective_id=0, has_side_effects=True),
    )(eigvecs, panels.reshape(SWEEPS, PIECE, B), sweep_shift, slot_group)


def solution(mesh):
    in_specs = (P("row", "col"), P(None, "row", "col", None), P(), P())
    return jax.shard_map(on_device, mesh=mesh, in_specs=in_specs, out_specs=P("row", "col"), check_vma=False)
```

```python
import jax
import jax.numpy as jnp
from jax import lax
from jax.experimental import pallas as pl
from jax.experimental.pallas import tpu as pltpu
from jax.sharding import PartitionSpec as P

MESH = pl.DeviceIdType.MESH
F32, BF16 = jnp.float32, jnp.bfloat16
B = 128
SWEEPS = 5
ROWS, COLS = 32, 8
RING = 8
PIECE = 32
WINDOWS = ((0, 0), (1, 0), (1, 1), (2, 0), (3, 0), (3, 1), (4, 0))
LATER = len(WINDOWS) - 1
CHUNK = 256
CHUNKS = 1024 // CHUNK
COPIES = 160


def split(a):
    high = a.astype(BF16)
    return high, (a - high.astype(F32)).astype(BF16)


def dot3(a, b, dims=((1,), (0,))):
    (ah, al), (bh, bl) = a, b
    dot = lambda x, y: lax.dot_general(x, y, (dims, ((), ())), preferred_element_type=F32)
    return dot(ah, bh) + (dot(ah, bl) + dot(al, bh))


def dot6(a, b, dims=((1,), (0,))):
    return lax.dot_general(a, b, (dims, ((), ())), precision=lax.Precision.HIGHEST, preferred_element_type=F32)


def inverses(grams):
    row = lax.broadcasted_iota(jnp.int32, (B, B), 0)
    col = lax.broadcasted_iota(jnp.int32, (B, B), 1)
    first = (col == row + 1) & ((row & 1) == 0)

    def start(gram):
        diagonal = jnp.where(row == col, gram, 0.0)
        down = 2.0 / jnp.sum(diagonal, axis=1, keepdims=True)
        along = 2.0 / jnp.sum(diagonal, axis=0, keepdims=True)
        return jnp.where(row == col, down, 0.0) - jnp.where(first, down * gram * along, 0.0)

    invs = [start(gram) for gram in grams]
    width = 2
    while width < B:
        pair = 2 * width
        corner = ((row & -pair) == (col & -pair)) & ((row & width) == 0) & ((col & width) != 0)
        offs = [jnp.where(corner, gram, 0.0) for gram in grams]
        if width < 8:
            inner = [dot6(inv, off) for inv, off in zip(invs, offs)]
            invs = [inv - dot6(part, inv) for part, inv in zip(inner, invs)]
        else:
            parts = [inv.reshape(B // pair, pair, B) for inv in invs]
            uppers = [part[:, :width].reshape(B // 2, B) for part in parts]
            inner = [dot6(upper, off) for upper, off in zip(uppers, offs)]
            uppers = [upper - dot6(part, inv) for upper, part, inv in zip(uppers, inner, invs)]
            invs = [
                jnp.concatenate([upper.reshape(B // pair, width, B), part[:, width:]], axis=1).reshape(B, B)
                for upper, part in zip(uppers, parts)
            ]
        width = pair
    return invs


def reflectors(panels):
    invs = inverses([dot6(panel, panel, ((0,), (0,))) for panel in panels])
    vs = [split(panel) for panel in panels]
    return [(v, dot3(v, split(inv))) for v, inv in zip(vs, invs)]


def transform(reflector, top):
    v, vt = reflector
    rows = slice(0, B) if top else slice(B, 2 * B)
    row = lax.broadcasted_iota(jnp.int32, (B, 2 * B), 0) + (0 if top else B)
    col = lax.broadcasted_iota(jnp.int32, (B, 2 * B), 1)
    return split(jnp.where(row == col, 1.0, 0.0) - dot3(split(vt[rows]), v, ((1,), (1,))))


def kernel(
    z_hbm, panels_hbm, shift, slots, out_hbm,
    z_in, panels, gathered0, gathered1, gathered2, gathered3, gathered4, stage, wanted0,
    far_out, far_in1, far_in2, far_in3, far_in4, full, blocks, outs, hh, hl, send_sem, recv_sem, own_sem,
):
    gathered, far_in = (gathered0, gathered1, gathered2, gathered3, gathered4), (far_in1, far_in2, far_in3, far_in4)
    r, c = lax.axis_index("row"), lax.axis_index("col")
    k = lax.rem(r, 2)
    z = lax.rem(lax.div(r, 2), RING)
    h = lax.div(r, 2 * RING)
    row_of = lambda h_, z_, k_: (h_ * RING + z_) * 2 + k_
    ring = lambda d: lax.rem(z + d + RING, RING)
    ring_row = lambda d: row_of(h, ring(d), k)
    mate, across = row_of(h, z, 1 - k), row_of(1 - h, z, k)
    prev_row, next_row = lax.rem(r + ROWS - 1, ROWS), lax.rem(r + 1, ROWS)
    other_col = lambda j: lax.rem(c + j + COLS, COLS)
    strip = lambda col: pl.ds(pl.multiple_of(col * PIECE, PIECE), PIECE)
    ids, sent = {}, []

    def remote(name, src, dst, row, col):
        i = ids.setdefault(name, len(ids))
        return pltpu.make_async_remote_copy(
            src_ref=src, dst_ref=dst, send_sem=send_sem.at[i], recv_sem=recv_sem.at[i],
            device_id=(row, col), device_id_type=MESH,
        )

    def send(name, src, dst, row, col):
        copy = remote(name, src, dst, row, col)
        copy.start()
        sent.append(copy)

    def arrive(name, dst):
        remote(name, dst, dst, mate, c).wait_recv()

    barrier = pltpu.get_barrier_semaphore()
    partners = [(ring_row(d), c) for d in range(1, RING)] + [(mate, c), (prev_row, c), (next_row, c)]
    everyone = [(flip, j) for flip in (0, 1) for j in range(COLS) if (flip, j) != (0, 0)]
    partners += [(across if flip else r, other_col(j)) for flip, j in everyone]
    for partner in partners:
        pl.semaphore_signal(barrier, inc=1, device_id=partner, device_id_type=MESH)
    panels_copy = pltpu.make_async_copy(panels_hbm, panels, own_sem.at[0])
    panels_copy.start()
    z_copy = pltpu.make_async_copy(z_hbm, z_in, own_sem.at[1])
    z_copy.start()
    pl.semaphore_wait(barrier, len(partners))
    panels_copy.wait()

    def ring_send(s):
        for d in (4, 3, 5, 2, 6, 1, 7):
            send(("ring", s, d), panels.at[s], gathered[s].at[k, z], ring_row(d), c)
        send(("mate", s, 0), panels.at[s], gathered[s].at[k, z], mate, c)

    def receive(s, distances):
        for d in distances:
            block = gathered[s].at[k, ring(-d)]
            arrive(("ring", s, d), block)
            send(("mate", s, d), block, block, mate, c)

    def receive_mate(s):
        for d in range(RING):
            arrive(("mate", s, d), gathered[s].at[1 - k, ring(-d)])

    near, distant = (1, 7, 2, 6), (3, 5, 4)
    ring_send(0)
    for s in range(SWEEPS):
        gathered[s][k, z] = panels[s]

    def find(s, row):
        wanted = lax.rem(row + 2 * ROWS - shift[s], ROWS)
        slot = jnp.int32(0)
        for p in range(ROWS):
            slot = jnp.where(slots[s, p] == wanted, p, slot)
        return lax.div(slot, 2 * RING), (lax.rem(slot, 2), lax.rem(lax.div(slot, 2), RING))

    halves, places = zip(*[find(s, r - back) for s, back in WINDOWS])
    _, places_across = zip(*[find(s, across - back) for s, back in WINDOWS])
    receive(0, near)
    ring_send(1)
    receive(0, distant)
    receive_mate(0)
    stage[0] = gathered[0][places[0]]
    far_out[0] = gathered[0][places_across[0]]
    wanted0[h, strip(c)] = gathered[0][places[0]]
    ring_send(2)
    for flip, j in everyone:
        source = far_out if flip else stage
        send(("first share", flip, j), source.at[0], wanted0.at[h, strip(c)], across if flip else r, other_col(j))

    of_sweep = [[w for w, (of, _) in enumerate(WINDOWS) if of == s] for s in range(SWEEPS)]

    def cross(s):
        receive_mate(s)
        ws = of_sweep[s]
        for w in ws:
            far_out[w] = gathered[s][places_across[w]]
        span = pl.ds(ws[0], len(ws))
        send(("far", s), far_out.at[span], far_in[s - 1].at[pl.ds(0, len(ws))], across, c)

    def share(s):
        ws = of_sweep[s]
        arrive(("far", s), far_in[s - 1].at[pl.ds(0, len(ws))])
        for i, w in enumerate(ws):
            piece = jnp.where(halves[w] == h, gathered[s][places[w]], far_in[s - 1][i])
            stage[w] = piece
            full[w - 1, strip(c)] = piece
        for w in ws:
            for j in range(1, COLS):
                send(("share", w, j), stage.at[w], full.at[w - 1, strip(c)], r, other_col(j))

    receive(1, near)
    ring_send(3)
    receive(1, distant)
    cross(1)
    receive(2, near)
    ring_send(4)
    receive(2, distant)
    cross(2)

    for flip, j in everyone:
        arrive(("first share", flip, j), wanted0.at[1 - h if flip else h, strip(other_col(-j))])
    share(1)
    (first,) = reflectors([wanted0[halves[0]]])
    hh[0, :B], hl[0, :B] = transform(first, True)
    hh[0, B:], hl[0, B:] = transform(first, False)
    share(2)
    receive(3, near + distant)
    cross(3)
    z_copy.wait()

    def times(s, rows, block):
        return dot3((hh[s, rows], hl[s, rows]), block)

    low, high, both = slice(0, B), slice(B, 2 * B), slice(0, 2 * B)

    def exchange(x, j):
        mine = blocks.at[x, j]
        send(("prev", x, j), mine.at[pl.ds(B, B)], mine.at[pl.ds(3 * B, B)], prev_row, c)
        send(("next", x, j), mine.at[pl.ds(2 * B, B)], mine.at[pl.ds(0, B)], next_row, c)

    def odd_even(x, j):
        s = 2 * x + 1
        mine = blocks.at[x, j]
        arrive(("prev", x, j), mine.at[pl.ds(3 * B, B)])
        arrive(("next", x, j), mine.at[pl.ds(0, B)])
        new_low = times(s, low, split(mine[0 : 2 * B]))
        new_high = times(s, high, split(mine[2 * B : 4 * B]))
        return times(s + 1, both, split(jnp.concatenate([new_low, new_high], axis=0)))

    def transforms(ws):
        s = WINDOWS[ws[0]][0]
        for w in ws:
            for j in range(1, COLS):
                arrive(("share", w, j), full.at[w - 1, strip(other_col(-j))])
        own, back, even = reflectors([full[w - 1] for w in ws])
        hh[s, low], hl[s, low] = transform(back, False)
        hh[s, high], hl[s, high] = transform(own, True)
        hh[s + 1, low], hl[s + 1, low] = transform(even, True)
        hh[s + 1, high], hl[s + 1, high] = transform(even, False)

    for j in range(CHUNKS):
        cols = slice(j * CHUNK, (j + 1) * CHUNK)
        blocks[0, j, B : 3 * B] = times(0, both, split(z_in[:, cols]))
        if j:
            exchange(0, j - 1)
    receive(4, near + distant)
    exchange(0, CHUNKS - 1)
    cross(4)
    share(3)
    transforms((1, 2, 3))
    share(4)
    for j in range(CHUNKS):
        blocks[1, j, B : 3 * B] = odd_even(0, j)
        if j:
            exchange(1, j - 1)
    z_in[0:8, 0:B] = jnp.zeros((8, B), F32)
    exchange(1, CHUNKS - 1)
    transforms((4, 5, 6))
    out_copies = []
    for j in range(CHUNKS):
        outs[j] = odd_even(1, j)
        cols = pl.ds(j * CHUNK, CHUNK)
        out_copies.append(pltpu.make_async_copy(outs.at[j], out_hbm.at[:, cols], own_sem.at[2 + j]))
        out_copies[-1].start()
    for copy in sent:
        copy.wait_send()
    for copy in out_copies:
        copy.wait()


def on_device(eigvecs, panels, sweep_shift, slot_group):
    rows, cols = eigvecs.shape
    hbm, smem = pl.BlockSpec(memory_space=pl.ANY), pl.BlockSpec(memory_space=pltpu.SMEM)
    return pl.pallas_call(
        kernel,
        out_shape=jax.ShapeDtypeStruct((rows, cols), F32),
        in_specs=[hbm, hbm, smem, smem],
        out_specs=hbm,
        scratch_shapes=[
            pltpu.VMEM((rows, cols), F32),
            pltpu.VMEM((SWEEPS, PIECE, B), F32),
            *[pltpu.VMEM((2, RING, PIECE, B), F32)] * SWEEPS,
            pltpu.VMEM((len(WINDOWS), PIECE, B), F32),
            pltpu.VMEM((2, 2 * B, B), F32),
            pltpu.VMEM((len(WINDOWS), PIECE, B), F32),
            *[pltpu.VMEM((2, PIECE, B), F32)] * (SWEEPS - 1),
            pltpu.VMEM((LATER, 2 * B, B), F32),
            pltpu.VMEM((2, CHUNKS, 4 * B, CHUNK), F32),
            pltpu.VMEM((CHUNKS, 2 * B, CHUNK), F32),
            pltpu.VMEM((SWEEPS, 2 * B, 2 * B), BF16),
            pltpu.VMEM((SWEEPS, 2 * B, 2 * B), BF16),
            pltpu.SemaphoreType.DMA((COPIES,)),
            pltpu.SemaphoreType.DMA((COPIES,)),
            pltpu.SemaphoreType.DMA((2 + CHUNKS,)),
        ],
        compiler_params=pltpu.CompilerParams(collective_id=0, has_side_effects=True),
    )(eigvecs, panels.reshape(SWEEPS, PIECE, B), sweep_shift, slot_group)


def solution(mesh):
    in_specs = (P("row", "col"), P(None, "row", "col", None), P(), P())
    return jax.shard_map(on_device, mesh=mesh, in_specs=in_specs, out_specs=P("row", "col"), check_vma=False)
```

```python
import jax
import jax.numpy as jnp
from jax import lax
from jax.experimental import pallas as pl
from jax.experimental.pallas import tpu as pltpu
from jax.sharding import PartitionSpec as P

MESH = pl.DeviceIdType.MESH
F32, BF16 = jnp.float32, jnp.bfloat16
B = 128
SWEEPS = 5
ROWS, COLS = 32, 8
RING = 8
PIECE = 32
WINDOWS = ((0, 0), (1, 0), (1, 1), (2, 0), (3, 0), (3, 1), (4, 0))
LATER = len(WINDOWS) - 1
CHUNK = 256
CHUNKS = 1024 // CHUNK
COPIES = 160


def split(a):
    high = a.astype(BF16)
    return high, (a - high.astype(F32)).astype(BF16)


def dot3(a, b, dims=((1,), (0,))):
    (ah, al), (bh, bl) = a, b
    dot = lambda x, y: lax.dot_general(x, y, (dims, ((), ())), preferred_element_type=F32)
    return dot(ah, bh) + (dot(ah, bl) + dot(al, bh))


def dot6(a, b, dims=((1,), (0,))):
    return lax.dot_general(a, b, (dims, ((), ())), precision=lax.Precision.HIGHEST, preferred_element_type=F32)


def inverses(grams, between=None):
    row = lax.broadcasted_iota(jnp.int32, (B, B), 0)
    col = lax.broadcasted_iota(jnp.int32, (B, B), 1)
    first = (col == row + 1) & ((row & 1) == 0)

    def start(gram):
        diagonal = jnp.where(row == col, gram, 0.0)
        down = 2.0 / jnp.sum(diagonal, axis=1, keepdims=True)
        along = 2.0 / jnp.sum(diagonal, axis=0, keepdims=True)
        return jnp.where(row == col, down, 0.0) - jnp.where(first, down * gram * along, 0.0)

    invs = [start(gram) for gram in grams]
    width = 2
    while width < B:
        pair = 2 * width
        corner = ((row & -pair) == (col & -pair)) & ((row & width) == 0) & ((col & width) != 0)
        offs = [jnp.where(corner, gram, 0.0) for gram in grams]
        if width < 8:
            inner = [dot3(split(inv), split(off)) for inv, off in zip(invs, offs)]
            invs = [inv - dot3(split(part), split(inv)) for part, inv in zip(inner, invs)]
        else:
            parts = [inv.reshape(B // pair, pair, B) for inv in invs]
            uppers = [part[:, :width].reshape(B // 2, B) for part in parts]
            inner = [dot3(split(upper), split(off)) for upper, off in zip(uppers, offs)]
            uppers = [upper - dot3(split(part), split(inv)) for upper, part, inv in zip(uppers, inner, invs)]
            invs = [
                jnp.concatenate([upper.reshape(B // pair, width, B), part[:, width:]], axis=1).reshape(B, B)
                for upper, part in zip(uppers, parts)
            ]
        width = pair
        if between and width == 16:
            between()
    return invs


def reflectors(panels, between=None):
    invs = inverses([dot6(panel, panel, ((0,), (0,))) for panel in panels], between)
    vs = [split(panel) for panel in panels]
    return [(v, dot3(v, split(inv))) for v, inv in zip(vs, invs)]


def transform(reflector, top):
    v, vt = reflector
    rows = slice(0, B) if top else slice(B, 2 * B)
    row = lax.broadcasted_iota(jnp.int32, (B, 2 * B), 0) + (0 if top else B)
    col = lax.broadcasted_iota(jnp.int32, (B, 2 * B), 1)
    return split(jnp.where(row == col, 1.0, 0.0) - dot3(split(vt[rows]), v, ((1,), (1,))))


def kernel(
    z_hbm, panels_hbm, shift, slots, out_hbm,
    z_in, panels, gathered0, gathered1, gathered2, gathered3, gathered4, stage, wanted0,
    far_out, far_in1, far_in2, far_in3, far_in4, full, blocks, outs, hh, hl, send_sem, recv_sem, own_sem,
):
    gathered, far_in = (gathered0, gathered1, gathered2, gathered3, gathered4), (far_in1, far_in2, far_in3, far_in4)
    r, c = lax.axis_index("row"), lax.axis_index("col")
    k = lax.rem(r, 2)
    z = lax.rem(lax.div(r, 2), RING)
    h = lax.div(r, 2 * RING)
    row_of = lambda h_, z_, k_: (h_ * RING + z_) * 2 + k_
    ring = lambda d: lax.rem(z + d + RING, RING)
    ring_row = lambda d: row_of(h, ring(d), k)
    mate, across = row_of(h, z, 1 - k), row_of(1 - h, z, k)
    prev_row, next_row = lax.rem(r + ROWS - 1, ROWS), lax.rem(r + 1, ROWS)
    other_col = lambda j: lax.rem(c + j + COLS, COLS)
    in_line = lambda col, j: lax.div(col, 4) * 4 + lax.rem(col + j + 4, 4)
    beside = lax.rem(c + 4, COLS)
    strip = lambda col: pl.ds(pl.multiple_of(col * PIECE, PIECE), PIECE)
    ids, sent = {}, []

    def remote(name, src, dst, row, col):
        i = ids.setdefault(name, len(ids))
        return pltpu.make_async_remote_copy(
            src_ref=src, dst_ref=dst, send_sem=send_sem.at[i], recv_sem=recv_sem.at[i],
            device_id=(row, col), device_id_type=MESH,
        )

    def send(name, src, dst, row, col):
        copy = remote(name, src, dst, row, col)
        copy.start()
        sent.append(copy)

    def arrive(name, dst):
        remote(name, dst, dst, mate, c).wait_recv()

    barrier = pltpu.get_barrier_semaphore()
    partners = [(ring_row(d), c) for d in range(1, RING)] + [(mate, c), (prev_row, c), (next_row, c)]
    everyone = [(flip, j) for flip in (0, 1) for j in range(COLS) if (flip, j) != (0, 0)]
    partners += [(across if flip else r, other_col(j)) for flip, j in everyone]
    for partner in partners:
        pl.semaphore_signal(barrier, inc=1, device_id=partner, device_id_type=MESH)
    panels_copy = pltpu.make_async_copy(panels_hbm, panels, own_sem.at[0])
    panels_copy.start()
    z_copy = pltpu.make_async_copy(z_hbm, z_in, own_sem.at[1])
    z_copy.start()
    pl.semaphore_wait(barrier, len(partners))
    panels_copy.wait()

    def ring_send(s):
        for d in (4, 3, 5, 2, 6, 1, 7):
            send(("ring", s, d), panels.at[s], gathered[s].at[k, z], ring_row(d), c)
        send(("mate", s, 0), panels.at[s], gathered[s].at[k, z], mate, c)

    def receive(s):
        for d in (1, 7, 2, 6, 3, 5, 4):
            block = gathered[s].at[k, ring(-d)]
            arrive(("ring", s, d), block)
            send(("mate", s, d), block, block, mate, c)

    def receive_mate(s):
        for d in range(RING):
            arrive(("mate", s, d), gathered[s].at[1 - k, ring(-d)])

    ring_send(0)
    ring_send(1)
    ring_send(2)
    for s in range(SWEEPS):
        gathered[s][k, z] = panels[s]

    def find(s, row):
        wanted = lax.rem(row + 2 * ROWS - shift[s], ROWS)
        slot = jnp.int32(0)
        for p in range(ROWS):
            slot = jnp.where(slots[s, p] == wanted, p, slot)
        return lax.div(slot, 2 * RING), (lax.rem(slot, 2), lax.rem(lax.div(slot, 2), RING))

    halves, places = zip(*[find(s, r - back) for s, back in WINDOWS])
    _, places_across = zip(*[find(s, across - back) for s, back in WINDOWS])
    receive(0)
    ring_send(3)
    receive_mate(0)
    stage[0] = gathered[0][places[0]]
    far_out[0] = gathered[0][places_across[0]]
    wanted0[h, strip(c)] = gathered[0][places[0]]
    for flip, j in everyone:
        source = far_out if flip else stage
        send(("first share", flip, j), source.at[0], wanted0.at[h, strip(c)], across if flip else r, other_col(j))

    of_sweep = [[w for w, (of, _) in enumerate(WINDOWS) if of == s] for s in range(SWEEPS)]

    def cross(s):
        receive_mate(s)
        ws = of_sweep[s]
        for w in ws:
            far_out[w] = gathered[s][places_across[w]]
        span = pl.ds(ws[0], len(ws))
        send(("far", s), far_out.at[span], far_in[s - 1].at[pl.ds(0, len(ws))], across, c)

    def share(s):
        ws = of_sweep[s]
        arrive(("far", s), far_in[s - 1].at[pl.ds(0, len(ws))])
        for i, w in enumerate(ws):
            piece = jnp.where(halves[w] == h, gathered[s][places[w]], far_in[s - 1][i])
            stage[w] = piece
            full[w - 1, strip(c)] = piece
        for w in ws:
            send(("beside", w), stage.at[w], full.at[w - 1, strip(c)], r, beside)
        for w in ws:
            for j in (1, 3, 2):
                send(("share", w, j), stage.at[w], full.at[w - 1, strip(c)], r, in_line(c, j))

    def relay(s):
        for w in of_sweep[s]:
            piece = full.at[w - 1, strip(beside)]
            arrive(("beside", w), piece)
            for j in (1, 3, 2):
                send(("relay", w, j), piece, piece, r, in_line(c, j))

    receive(1)
    ring_send(4)
    cross(1)
    receive(2)
    cross(2)
    for flip, j in everyone:
        arrive(("first share", flip, j), wanted0.at[1 - h if flip else h, strip(other_col(-j))])
    (first,) = reflectors([wanted0[halves[0]]], lambda: share(1))
    share(2)
    hh[0, :B], hl[0, :B] = transform(first, True)
    hh[0, B:], hl[0, B:] = transform(first, False)
    receive(3)
    relay(1)
    z_copy.wait()

    def times(s, rows, block):
        return dot3((hh[s, rows], hl[s, rows]), block)

    low, high, both = slice(0, B), slice(B, 2 * B), slice(0, 2 * B)

    def exchange(x, j):
        mine = blocks.at[x, j]
        send(("prev", x, j), mine.at[pl.ds(B, B)], mine.at[pl.ds(3 * B, B)], prev_row, c)
        send(("next", x, j), mine.at[pl.ds(2 * B, B)], mine.at[pl.ds(0, B)], next_row, c)

    def odd_even(x, j):
        s = 2 * x + 1
        mine = blocks.at[x, j]
        arrive(("prev", x, j), mine.at[pl.ds(3 * B, B)])
        arrive(("next", x, j), mine.at[pl.ds(0, B)])
        new_low = times(s, low, split(mine[0 : 2 * B]))
        new_high = times(s, high, split(mine[2 * B : 4 * B]))
        return times(s + 1, both, split(jnp.concatenate([new_low, new_high], axis=0)))

    def await_shares(ws):
        for w in ws:
            for j in (1, 3, 2):
                arrive(("share", w, j), full.at[w - 1, strip(in_line(c, -j))])
                arrive(("relay", w, j), full.at[w - 1, strip(in_line(beside, -j))])

    def transforms(ws):
        s = WINDOWS[ws[0]][0]
        own, back, even = reflectors([full[w - 1] for w in ws])
        hh[s, low], hl[s, low] = transform(back, False)
        hh[s, high], hl[s, high] = transform(own, True)
        hh[s + 1, low], hl[s + 1, low] = transform(even, True)
        hh[s + 1, high], hl[s + 1, high] = transform(even, False)

    for j in range(CHUNKS):
        cols = slice(j * CHUNK, (j + 1) * CHUNK)
        blocks[0, j, B : 3 * B] = times(0, both, split(z_in[:, cols]))
        if j == 0:
            relay(2)
        if j == 1:
            cross(3)
        if j:
            exchange(0, j - 1)
        if j == 2:
            receive(4)
    cross(4)
    exchange(0, CHUNKS - 1)
    await_shares((1, 2, 3))
    transforms((1, 2, 3))
    share(3)
    share(4)
    for j in range(CHUNKS):
        blocks[1, j, B : 3 * B] = odd_even(0, j)
        if j < 2:
            relay(3 + j)
        if j:
            exchange(1, j - 1)
    z_in[0:8, 0:B] = jnp.zeros((8, B), F32)
    exchange(1, CHUNKS - 1)
    await_shares((4, 5, 6))
    transforms((4, 5, 6))
    out_copies = []
    for j in range(CHUNKS):
        outs[j] = odd_even(1, j)
        cols = pl.ds(j * CHUNK, CHUNK)
        out_copies.append(pltpu.make_async_copy(outs.at[j], out_hbm.at[:, cols], own_sem.at[2 + j]))
        out_copies[-1].start()
    for copy in sent:
        copy.wait_send()
    for copy in out_copies:
        copy.wait()


def on_device(eigvecs, panels, sweep_shift, slot_group):
    rows, cols = eigvecs.shape
    hbm, smem = pl.BlockSpec(memory_space=pl.ANY), pl.BlockSpec(memory_space=pltpu.SMEM)
    return pl.pallas_call(
        kernel,
        out_shape=jax.ShapeDtypeStruct((rows, cols), F32),
        in_specs=[hbm, hbm, smem, smem],
        out_specs=hbm,
        scratch_shapes=[
            pltpu.VMEM((rows, cols), F32),
            pltpu.VMEM((SWEEPS, PIECE, B), F32),
            *[pltpu.VMEM((2, RING, PIECE, B), F32)] * SWEEPS,
            pltpu.VMEM((len(WINDOWS), PIECE, B), F32),
            pltpu.VMEM((2, 2 * B, B), F32),
            pltpu.VMEM((len(WINDOWS), PIECE, B), F32),
            *[pltpu.VMEM((2, PIECE, B), F32)] * (SWEEPS - 1),
            pltpu.VMEM((LATER, 2 * B, B), F32),
            pltpu.VMEM((2, CHUNKS, 4 * B, CHUNK), F32),
            pltpu.VMEM((CHUNKS, 2 * B, CHUNK), F32),
            pltpu.VMEM((SWEEPS, 2 * B, 2 * B), BF16),
            pltpu.VMEM((SWEEPS, 2 * B, 2 * B), BF16),
            pltpu.SemaphoreType.DMA((COPIES,)),
            pltpu.SemaphoreType.DMA((COPIES,)),
            pltpu.SemaphoreType.DMA((2 + CHUNKS,)),
        ],
        compiler_params=pltpu.CompilerParams(collective_id=0, has_side_effects=True),
    )(eigvecs, panels.reshape(SWEEPS, PIECE, B), sweep_shift, slot_group)


def solution(mesh):
    in_specs = (P("row", "col"), P(None, "row", "col", None), P(), P())
    return jax.shard_map(on_device, mesh=mesh, in_specs=in_specs, out_specs=P("row", "col"), check_vma=False)
```

```python
import jax
import jax.numpy as jnp
from jax import lax
from jax.experimental import pallas as pl
from jax.experimental.pallas import tpu as pltpu
from jax.sharding import PartitionSpec as P

MESH = pl.DeviceIdType.MESH
F32, BF16 = jnp.float32, jnp.bfloat16
B = 128
SWEEPS = 5
ROWS, COLS = 32, 8
RING = 8
PIECE = 32
WINDOWS = ((0, 0), (1, 0), (1, 1), (2, 0), (3, 0), (3, 1), (4, 0))
CHUNK = 256
CHUNKS = 1024 // CHUNK
COPIES = 130


def split(a):
    high = a.astype(BF16)
    return high, (a - high.astype(F32)).astype(BF16)


def dot3(a, b, dims=((1,), (0,))):
    (ah, al), (bh, bl) = a, b
    dot = lambda x, y: lax.dot_general(x, y, (dims, ((), ())), preferred_element_type=F32)
    return dot(ah, bh) + (dot(ah, bl) + dot(al, bh))


def dot6(a, b, dims=((1,), (0,))):
    return lax.dot_general(a, b, (dims, ((), ())), precision=lax.Precision.HIGHEST, preferred_element_type=F32)


def inverses(grams, between=None):
    row = lax.broadcasted_iota(jnp.int32, (B, B), 0)
    col = lax.broadcasted_iota(jnp.int32, (B, B), 1)
    first = (col == row + 1) & ((row & 1) == 0)

    def start(gram):
        diagonal = jnp.where(row == col, gram, 0.0)
        down = 2.0 / jnp.sum(diagonal, axis=1, keepdims=True)
        along = 2.0 / jnp.sum(diagonal, axis=0, keepdims=True)
        return jnp.where(row == col, down, 0.0) - jnp.where(first, down * gram * along, 0.0)

    invs = [start(gram) for gram in grams]
    width = 2
    while width < B:
        pair = 2 * width
        corner = ((row & -pair) == (col & -pair)) & ((row & width) == 0) & ((col & width) != 0)
        offs = [jnp.where(corner, gram, 0.0) for gram in grams]
        if width < 8:
            inner = [dot3(split(inv), split(off)) for inv, off in zip(invs, offs)]
            invs = [inv - dot3(split(part), split(inv)) for part, inv in zip(inner, invs)]
        else:
            parts = [inv.reshape(B // pair, pair, B) for inv in invs]
            uppers = [part[:, :width].reshape(B // 2, B) for part in parts]
            inner = [dot3(split(upper), split(off)) for upper, off in zip(uppers, offs)]
            uppers = [upper - dot3(split(part), split(inv)) for upper, part, inv in zip(uppers, inner, invs)]
            invs = [
                jnp.concatenate([upper.reshape(B // pair, width, B), part[:, width:]], axis=1).reshape(B, B)
                for upper, part in zip(uppers, parts)
            ]
        width = pair
        if between and width == 16:
            between()
    return invs


def reflectors(panels, between=None):
    invs = inverses([dot6(panel, panel, ((0,), (0,))) for panel in panels], between)
    vs = [split(panel) for panel in panels]
    return [(v, dot3(v, split(inv))) for v, inv in zip(vs, invs)]


def transform(reflector, top):
    v, vt = reflector
    rows = slice(0, B) if top else slice(B, 2 * B)
    row = lax.broadcasted_iota(jnp.int32, (B, 2 * B), 0) + (0 if top else B)
    col = lax.broadcasted_iota(jnp.int32, (B, 2 * B), 1)
    return split(jnp.where(row == col, 1.0, 0.0) - dot3(split(vt[rows]), v, ((1,), (1,))))


def kernel(
    z_hbm, panels_hbm, shift, slots, out_hbm,
    z_in, panels, gathered0, gathered1, gathered2, gathered3, gathered4, near, far, along_x, pair, full,
    blocks, outs, hh, hl, send_sem, recv_sem, own_sem,
):
    gathered = gathered0, gathered1, gathered2, gathered3, gathered4
    r, c = lax.axis_index("row"), lax.axis_index("col")
    k = lax.rem(r, 2)
    z = lax.rem(lax.div(r, 2), RING)
    h = lax.div(r, 2 * RING)
    row_of = lambda h_, z_, k_: (h_ * RING + z_) * 2 + k_
    ring = lambda d: lax.rem(z + d + RING, RING)
    ring_row = lambda d: row_of(h, ring(d), k)
    mate, across = row_of(h, z, 1 - k), row_of(1 - h, z, k)
    prev_row, next_row = lax.rem(r + ROWS - 1, ROWS), lax.rem(r + 1, ROWS)
    x, y = lax.div(c, 4), lax.rem(c, 4)
    in_line = lambda j: lax.rem(y + j + 4, 4)
    beside = lax.rem(c + 4, COLS)
    ids, sent = {}, []

    def remote(name, src, dst, row, col):
        i = ids.setdefault(name, len(ids))
        return pltpu.make_async_remote_copy(
            src_ref=src, dst_ref=dst, send_sem=send_sem.at[i], recv_sem=recv_sem.at[i],
            device_id=(row, col), device_id_type=MESH,
        )

    def send(name, src, dst, row, col):
        copy = remote(name, src, dst, row, col)
        copy.start()
        sent.append(copy)

    def arrive(name, dst):
        remote(name, dst, dst, mate, c).wait_recv()

    barrier = pltpu.get_barrier_semaphore()
    partners = [(ring_row(d), c) for d in range(1, RING)] + [(mate, c), (prev_row, c), (next_row, c)]
    partners += [(r, beside), (across, c), (across, beside)] + [(r, x * 4 + in_line(j)) for j in (1, 2, 3)]
    for partner in partners:
        pl.semaphore_signal(barrier, inc=1, device_id=partner, device_id_type=MESH)
    panels_copy = pltpu.make_async_copy(panels_hbm, panels, own_sem.at[0])
    panels_copy.start()
    z_copy = pltpu.make_async_copy(z_hbm, z_in, own_sem.at[1])
    z_copy.start()
    pl.semaphore_wait(barrier, len(partners))
    panels_copy.wait()

    def ring_send(s, distances):
        for d in distances:
            send(("ring", s, d), panels.at[s], gathered[s].at[k, z], ring_row(d), c)
        send(("mate", s, 0), panels.at[s], gathered[s].at[k, z], mate, c)

    def receive(s, distances):
        for d in distances:
            block = gathered[s].at[k, ring(-d)]
            arrive(("ring", s, d), block)
            send(("mate", s, d), block, block, mate, c)

    def pass_on(s):
        receive(s, (2, 6))
        for d, origin, target in ((3, -2, 1), (5, 2, -1), (4, 4 * k - 2, 2 - 4 * k)):
            block = gathered[s].at[k, ring(origin)]
            send(("ring", s, d), block, block, ring_row(target), c)
        receive(s, (1, 7))

    straight, nearest, rest = (4, 3, 5, 2, 6, 1, 7), (2, 6, 1, 7), (3, 5, 4)

    def receive_mate(s):
        for d in range(RING):
            arrive(("mate", s, d), gathered[s].at[1 - k, ring(-d)])

    ring_send(0, straight)
    ring_send(1, nearest)
    ring_send(2, nearest)
    for s in range(SWEEPS):
        gathered[s][k, z] = panels[s]

    def find(s, row):
        wanted = lax.rem(row + 2 * ROWS - shift[s], ROWS)
        slot = jnp.int32(0)
        for p in range(ROWS):
            slot = jnp.where(slots[s, p] == wanted, p, slot)
        return lax.div(slot, 2 * RING), (lax.rem(slot, 2), lax.rem(lax.div(slot, 2), RING))

    halves, places = zip(*[find(s, r - back) for s, back in WINDOWS])
    _, places_across = zip(*[find(s, across - back) for s, back in WINDOWS])
    of_sweep = [[w for w, (of, _) in enumerate(WINDOWS) if of == s] for s in range(SWEEPS)]
    span = [pl.ds(ws[0], len(ws)) for ws in of_sweep]

    def spread(s):
        receive_mate(s)
        for w in of_sweep[s]:
            near[w] = gathered[s][places[w]]
            far[w] = gathered[s][places_across[w]]
        send(("near", s), near.at[span[s]], along_x.at[0, span[s]], r, beside)
        send(("far", s), far.at[span[s]], along_x.at[1, span[s]], across, c)
        send(("far beside", s), far.at[span[s]], along_x.at[2, span[s]], across, beside)

    def share(s):
        for i, name in enumerate(("near", "far", "far beside")):
            arrive((name, s), along_x.at[i, span[s]])
        for w in of_sweep[s]:
            here = halves[w] == h
            for of_x, piece in (
                (x, jnp.where(here, near[w], along_x[1, w])),
                (1 - x, jnp.where(here, along_x[0, w], along_x[2, w])),
            ):
                pair[w, of_x] = piece
                full[w, of_x, y] = piece
        for j in (1, 3, 2):
            send(("share", s, j), pair.at[span[s]], full.at[span[s], :, y], r, x * 4 + in_line(j))

    def await_share(s):
        for j in (1, 3, 2):
            arrive(("share", s, j), full.at[span[s], :, in_line(-j)])

    receive(0, (1, 7, 2, 6, 3, 5, 4))
    pass_on(1)
    pass_on(2)
    ring_send(3, nearest)
    ring_send(4, nearest)
    spread(0)
    receive(1, rest)
    spread(1)
    share(0)
    receive(2, rest)
    spread(2)
    pass_on(3)
    pass_on(4)
    share(1)
    receive(3, rest)
    receive(4, rest)
    await_share(0)

    def between():
        share(2)
        spread(3)
        spread(4)

    (first,) = reflectors([full[0].reshape(2 * B, B)], between)
    hh[0, :B], hl[0, :B] = transform(first, True)
    hh[0, B:], hl[0, B:] = transform(first, False)
    z_copy.wait()

    def times(s, rows, block):
        return dot3((hh[s, rows], hl[s, rows]), block)

    low, high, both = slice(0, B), slice(B, 2 * B), slice(0, 2 * B)

    def exchange(x, j):
        mine = blocks.at[x, j]
        send(("prev", x, j), mine.at[pl.ds(B, B)], mine.at[pl.ds(3 * B, B)], prev_row, c)
        send(("next", x, j), mine.at[pl.ds(2 * B, B)], mine.at[pl.ds(0, B)], next_row, c)

    def odd_even(x, j):
        s = 2 * x + 1
        mine = blocks.at[x, j]
        arrive(("prev", x, j), mine.at[pl.ds(3 * B, B)])
        arrive(("next", x, j), mine.at[pl.ds(0, B)])
        new_low = times(s, low, split(mine[0 : 2 * B]))
        new_high = times(s, high, split(mine[2 * B : 4 * B]))
        return times(s + 1, both, split(jnp.concatenate([new_low, new_high], axis=0)))

    def transforms(ws):
        s = WINDOWS[ws[0]][0]
        own, back, even = reflectors([full[w].reshape(2 * B, B) for w in ws])
        hh[s, low], hl[s, low] = transform(back, False)
        hh[s, high], hl[s, high] = transform(own, True)
        hh[s + 1, low], hl[s + 1, low] = transform(even, True)
        hh[s + 1, high], hl[s + 1, high] = transform(even, False)

    for j in range(CHUNKS):
        cols = slice(j * CHUNK, (j + 1) * CHUNK)
        blocks[0, j, B : 3 * B] = times(0, both, split(z_in[:, cols]))
        if j:
            exchange(0, j - 1)
    await_share(1)
    exchange(0, CHUNKS - 1)
    await_share(2)
    transforms((1, 2, 3))
    for j in range(CHUNKS):
        blocks[1, j, B : 3 * B] = odd_even(0, j)
        if j:
            exchange(1, j - 1)
        if j in (1, 2):
            share(j + 2)
    z_in[0:8, 0:B] = jnp.zeros((8, B), F32)
    exchange(1, CHUNKS - 1)
    await_share(3)
    await_share(4)
    transforms((4, 5, 6))
    out_copies = []
    for j in range(CHUNKS):
        outs[j] = odd_even(1, j)
        cols = pl.ds(j * CHUNK, CHUNK)
        out_copies.append(pltpu.make_async_copy(outs.at[j], out_hbm.at[:, cols], own_sem.at[2 + j]))
        out_copies[-1].start()
    for copy in sent:
        copy.wait_send()
    for copy in out_copies:
        copy.wait()


def on_device(eigvecs, panels, sweep_shift, slot_group):
    rows, cols = eigvecs.shape
    hbm, smem = pl.BlockSpec(memory_space=pl.ANY), pl.BlockSpec(memory_space=pltpu.SMEM)
    return pl.pallas_call(
        kernel,
        out_shape=jax.ShapeDtypeStruct((rows, cols), F32),
        in_specs=[hbm, hbm, smem, smem],
        out_specs=hbm,
        scratch_shapes=[
            pltpu.VMEM((rows, cols), F32),
            pltpu.VMEM((SWEEPS, PIECE, B), F32),
            *[pltpu.VMEM((2, RING, PIECE, B), F32)] * SWEEPS,
            pltpu.VMEM((len(WINDOWS), PIECE, B), F32),
            pltpu.VMEM((len(WINDOWS), PIECE, B), F32),
            pltpu.VMEM((3, len(WINDOWS), PIECE, B), F32),
            pltpu.VMEM((len(WINDOWS), 2, PIECE, B), F32),
            pltpu.VMEM((len(WINDOWS), 2, 4, PIECE, B), F32),
            pltpu.VMEM((2, CHUNKS, 4 * B, CHUNK), F32),
            pltpu.VMEM((CHUNKS, 2 * B, CHUNK), F32),
            pltpu.VMEM((SWEEPS, 2 * B, 2 * B), BF16),
            pltpu.VMEM((SWEEPS, 2 * B, 2 * B), BF16),
            pltpu.SemaphoreType.DMA((COPIES,)),
            pltpu.SemaphoreType.DMA((COPIES,)),
            pltpu.SemaphoreType.DMA((2 + CHUNKS,)),
        ],
        compiler_params=pltpu.CompilerParams(collective_id=0, has_side_effects=True),
    )(eigvecs, panels.reshape(SWEEPS, PIECE, B), sweep_shift, slot_group)


def solution(mesh):
    in_specs = (P("row", "col"), P(None, "row", "col", None), P(), P())
    return jax.shard_map(on_device, mesh=mesh, in_specs=in_specs, out_specs=P("row", "col"), check_vma=False)
```

```python
import jax
import jax.numpy as jnp
from jax import lax
from jax.experimental import pallas as pl
from jax.experimental.pallas import tpu as pltpu
from jax.sharding import PartitionSpec as P

MESH = pl.DeviceIdType.MESH
F32, BF16 = jnp.float32, jnp.bfloat16
B = 128
SWEEPS = 5
ROWS, COLS = 32, 8
RING = 8
PIECE = 32
WINDOWS = ((0, 0), (1, 0), (1, 1), (2, 0), (3, 0), (3, 1), (4, 0))
CHUNK = 256
CHUNKS = 1024 // CHUNK
COPIES = 130


def split(a):
    high = a.astype(BF16)
    return high, (a - high.astype(F32)).astype(BF16)


def dot3(a, b, dims=((1,), (0,))):
    (ah, al), (bh, bl) = a, b
    dot = lambda x, y: lax.dot_general(x, y, (dims, ((), ())), preferred_element_type=F32)
    return dot(ah, bh) + (dot(ah, bl) + dot(al, bh))


def dot6(a, b, dims=((1,), (0,))):
    return lax.dot_general(a, b, (dims, ((), ())), precision=lax.Precision.HIGHEST, preferred_element_type=F32)


def inverses(grams, between):
    row = lax.broadcasted_iota(jnp.int32, (B, B), 0)
    col = lax.broadcasted_iota(jnp.int32, (B, B), 1)
    first = (col == row + 1) & ((row & 1) == 0)

    def start(gram):
        diagonal = jnp.where(row == col, gram, 0.0)
        down = 2.0 / jnp.sum(diagonal, axis=1, keepdims=True)
        along = 2.0 / jnp.sum(diagonal, axis=0, keepdims=True)
        return jnp.where(row == col, down, 0.0) - jnp.where(first, down * gram * along, 0.0)

    invs = [start(gram) for gram in grams]
    width = 2
    while width < B:
        pair = 2 * width
        corner = ((row & -pair) == (col & -pair)) & ((row & width) == 0) & ((col & width) != 0)
        offs = [jnp.where(corner, gram, 0.0) for gram in grams]
        if width < 8:
            inner = [dot3(split(inv), split(off)) for inv, off in zip(invs, offs)]
            invs = [inv - dot3(split(part), split(inv)) for part, inv in zip(inner, invs)]
        else:
            parts = [inv.reshape(B // pair, pair, B) for inv in invs]
            uppers = [part[:, :width].reshape(B // 2, B) for part in parts]
            inner = [dot3(split(upper), split(off)) for upper, off in zip(uppers, offs)]
            uppers = [upper - dot3(split(part), split(inv)) for upper, part, inv in zip(uppers, inner, invs)]
            invs = [
                jnp.concatenate([upper.reshape(B // pair, width, B), part[:, width:]], axis=1).reshape(B, B)
                for upper, part in zip(uppers, parts)
            ]
        width = pair
        between.get(width, lambda: None)()
    return invs


def reflectors(panels, between):
    invs = inverses([dot6(panel, panel, ((0,), (0,))) for panel in panels], between)
    vs = [split(panel) for panel in panels]
    return [(v, dot3(v, split(inv))) for v, inv in zip(vs, invs)]


def transform(reflector, top):
    v, vt = reflector
    rows = slice(0, B) if top else slice(B, 2 * B)
    row = lax.broadcasted_iota(jnp.int32, (B, 2 * B), 0) + (0 if top else B)
    col = lax.broadcasted_iota(jnp.int32, (B, 2 * B), 1)
    return split(jnp.where(row == col, 1.0, 0.0) - dot3(split(vt[rows]), v, ((1,), (1,))))


def kernel(
    z_hbm, panels_hbm, shift, slots, out_ref,
    z_in, panels, gathered0, gathered1, gathered2, gathered3, gathered4, near, far, along_x, pair, full,
    blocks, hh, hl, send_sem, recv_sem, own_sem,
):
    gathered = gathered0, gathered1, gathered2, gathered3, gathered4
    r, c = lax.axis_index("row"), lax.axis_index("col")
    k = lax.rem(r, 2)
    z = lax.rem(lax.div(r, 2), RING)
    h = lax.div(r, 2 * RING)
    row_of = lambda h_, z_, k_: (h_ * RING + z_) * 2 + k_
    ring = lambda d: lax.rem(z + d + RING, RING)
    ring_row = lambda d: row_of(h, ring(d), k)
    mate, across = row_of(h, z, 1 - k), row_of(1 - h, z, k)
    prev_row, next_row = lax.rem(r + ROWS - 1, ROWS), lax.rem(r + 1, ROWS)
    x, y = lax.div(c, 4), lax.rem(c, 4)
    in_line = lambda j: lax.rem(y + j + 4, 4)
    beside = lax.rem(c + 4, COLS)
    ids, sent = {}, []

    def remote(name, src, dst, row, col):
        i = ids.setdefault(name, len(ids))
        return pltpu.make_async_remote_copy(
            src_ref=src, dst_ref=dst, send_sem=send_sem.at[i], recv_sem=recv_sem.at[i],
            device_id=(row, col), device_id_type=MESH,
        )

    def send(name, src, dst, row, col):
        copy = remote(name, src, dst, row, col)
        copy.start()
        sent.append(copy)

    def arrive(name, dst):
        remote(name, dst, dst, mate, c).wait_recv()

    barrier = pltpu.get_barrier_semaphore()
    partners = [(ring_row(d), c) for d in range(1, RING)] + [(mate, c), (prev_row, c), (next_row, c)]
    partners += [(r, beside), (across, c), (across, beside)] + [(r, x * 4 + in_line(j)) for j in (1, 2, 3)]
    for partner in partners:
        pl.semaphore_signal(barrier, inc=1, device_id=partner, device_id_type=MESH)
    panels_copy = pltpu.make_async_copy(panels_hbm, panels, own_sem.at[0])
    panels_copy.start()
    z_copy = pltpu.make_async_copy(z_hbm, z_in, own_sem.at[1])
    z_copy.start()
    pl.semaphore_wait(barrier, len(partners))
    panels_copy.wait()

    def ring_send(s, distances):
        for d in distances:
            send(("ring", s, d), panels.at[s], gathered[s].at[k, z], ring_row(d), c)
        send(("mate", s, 0), panels.at[s], gathered[s].at[k, z], mate, c)

    def receive(s, distances):
        for d in distances:
            block = gathered[s].at[k, ring(-d)]
            arrive(("ring", s, d), block)
            send(("mate", s, d), block, block, mate, c)

    def pass_on(s):
        receive(s, (2, 6))
        for d, origin, target in ((3, -2, 1), (5, 2, -1), (4, 4 * k - 2, 2 - 4 * k)):
            block = gathered[s].at[k, ring(origin)]
            send(("ring", s, d), block, block, ring_row(target), c)
        receive(s, (1, 7))

    straight, nearest, rest = (4, 3, 5, 2, 6, 1, 7), (2, 6, 1, 7), (3, 5, 4)

    def receive_mate(s):
        for d in range(RING):
            arrive(("mate", s, d), gathered[s].at[1 - k, ring(-d)])

    ring_send(0, straight)
    ring_send(1, nearest)
    ring_send(2, nearest)
    for s in range(SWEEPS):
        gathered[s][k, z] = panels[s]

    def find(s, row):
        wanted = lax.rem(row + 2 * ROWS - shift[s], ROWS)
        slot = jnp.int32(0)
        for p in range(ROWS):
            slot = jnp.where(slots[s, p] == wanted, p, slot)
        return lax.div(slot, 2 * RING), (lax.rem(slot, 2), lax.rem(lax.div(slot, 2), RING))

    halves, places = zip(*[find(s, r - back) for s, back in WINDOWS])
    _, places_across = zip(*[find(s, across - back) for s, back in WINDOWS])
    def windows_of(*sweeps):
        ws = [w for w, (of, _) in enumerate(WINDOWS) if of in sweeps]
        return ws, pl.ds(ws[0], len(ws))

    def spread(*sweeps):
        ws, span = windows_of(*sweeps)
        for s in sweeps:
            receive_mate(s)
        for w in ws:
            s = WINDOWS[w][0]
            near[w] = gathered[s][places[w]]
            far[w] = gathered[s][places_across[w]]
        send(("far", sweeps), far.at[span], along_x.at[1, span], across, c)
        send(("far beside", sweeps), far.at[span], along_x.at[2, span], across, beside)
        send(("near", sweeps), near.at[span], along_x.at[0, span], r, beside)

    def share(*sweeps):
        ws, span = windows_of(*sweeps)
        for i, name in enumerate(("near", "far", "far beside")):
            arrive((name, sweeps), along_x.at[i, span])
        for w in ws:
            here = halves[w] == h
            for of_x, piece in (
                (x, jnp.where(here, near[w], along_x[1, w])),
                (1 - x, jnp.where(here, along_x[0, w], along_x[2, w])),
            ):
                pair[w, of_x] = piece
                full[w, of_x, y] = piece
        for j in (2, 1, 3):
            send(("share", sweeps, j), pair.at[span], full.at[span, :, y], r, x * 4 + in_line(j))

    def await_share(*sweeps):
        _, span = windows_of(*sweeps)
        for j in (1, 3, 2):
            arrive(("share", sweeps, j), full.at[span, :, in_line(-j)])

    receive(0, (1, 7, 2, 6))
    ring_send(3, nearest)
    ring_send(4, nearest)
    pass_on(1)
    receive(0, rest)
    pass_on(2)
    spread(0)
    receive(1, rest)
    pass_on(3)
    pass_on(4)
    spread(1)
    share(0)
    receive(2, rest)
    spread(2)
    share(1)
    receive(3, rest)
    receive(4, rest)
    await_share(0)

    def halfway():
        share(2)
        spread(3, 4)

    (first,) = reflectors([full[0].reshape(2 * B, B)], {16: halfway})
    hh[0, :B], hl[0, :B] = transform(first, True)
    hh[0, B:], hl[0, B:] = transform(first, False)
    z_copy.wait()

    def times(s, rows, block):
        return dot3((hh[s, rows], hl[s, rows]), block)

    low, high, both = slice(0, B), slice(B, 2 * B), slice(0, 2 * B)

    def exchange(x, j):
        mine = blocks.at[x, j]
        send(("prev", x, j), mine.at[pl.ds(B, B)], mine.at[pl.ds(3 * B, B)], prev_row, c)
        send(("next", x, j), mine.at[pl.ds(2 * B, B)], mine.at[pl.ds(0, B)], next_row, c)

    def odd_even(x, j):
        s = 2 * x + 1
        mine = blocks.at[x, j]
        arrive(("prev", x, j), mine.at[pl.ds(3 * B, B)])
        arrive(("next", x, j), mine.at[pl.ds(0, B)])
        new_low = times(s, low, split(mine[0 : 2 * B]))
        new_high = times(s, high, split(mine[2 * B : 4 * B]))
        return times(s + 1, both, split(jnp.concatenate([new_low, new_high], axis=0)))

    def transforms(ws, between={}):
        s = WINDOWS[ws[0]][0]
        own, back, even = reflectors([full[w].reshape(2 * B, B) for w in ws], between)
        hh[s, low], hl[s, low] = transform(back, False)
        hh[s, high], hl[s, high] = transform(own, True)
        hh[s + 1, low], hl[s + 1, low] = transform(even, True)
        hh[s + 1, high], hl[s + 1, high] = transform(even, False)

    for j in range(CHUNKS):
        cols = slice(j * CHUNK, (j + 1) * CHUNK)
        blocks[0, j, B : 3 * B] = times(0, both, split(z_in[:, cols]))
        if j:
            exchange(0, j - 1)
    await_share(1)
    exchange(0, CHUNKS - 1)
    share(3, 4)
    await_share(2)
    transforms((1, 2, 3))
    for j in range(CHUNKS):
        blocks[1, j, B : 3 * B] = odd_even(0, j)
        if j:
            exchange(1, j - 1)
    z_in[0:8, 0:B] = jnp.zeros((8, B), F32)
    exchange(1, CHUNKS - 1)
    await_share(3, 4)
    transforms((4, 5, 6))
    for j in range(CHUNKS):
        out_ref[:, j * CHUNK : (j + 1) * CHUNK] = odd_even(1, j)
    for copy in sent:
        copy.wait_send()


def on_device(eigvecs, panels, sweep_shift, slot_group):
    rows, cols = eigvecs.shape
    hbm, smem = pl.BlockSpec(memory_space=pl.ANY), pl.BlockSpec(memory_space=pltpu.SMEM)
    return pl.pallas_call(
        kernel,
        out_shape=pltpu.VMEM((rows, cols), F32),
        in_specs=[hbm, hbm, smem, smem],
        out_specs=pl.BlockSpec(memory_space=pltpu.VMEM),
        scratch_shapes=[
            pltpu.VMEM((rows, cols), F32),
            pltpu.VMEM((SWEEPS, PIECE, B), F32),
            *[pltpu.VMEM((2, RING, PIECE, B), F32)] * SWEEPS,
            pltpu.VMEM((len(WINDOWS), PIECE, B), F32),
            pltpu.VMEM((len(WINDOWS), PIECE, B), F32),
            pltpu.VMEM((3, len(WINDOWS), PIECE, B), F32),
            pltpu.VMEM((len(WINDOWS), 2, PIECE, B), F32),
            pltpu.VMEM((len(WINDOWS), 2, 4, PIECE, B), F32),
            pltpu.VMEM((2, CHUNKS, 4 * B, CHUNK), F32),
            pltpu.VMEM((SWEEPS, 2 * B, 2 * B), BF16),
            pltpu.VMEM((SWEEPS, 2 * B, 2 * B), BF16),
            pltpu.SemaphoreType.DMA((COPIES,)),
            pltpu.SemaphoreType.DMA((COPIES,)),
            pltpu.SemaphoreType.DMA((2,)),
        ],
        compiler_params=pltpu.CompilerParams(collective_id=0, has_side_effects=True),
    )(eigvecs, panels.reshape(SWEEPS, PIECE, B), sweep_shift, slot_group)


def solution(mesh):
    in_specs = (P("row", "col"), P(None, "row", "col", None), P(), P())
    return jax.shard_map(on_device, mesh=mesh, in_specs=in_specs, out_specs=P("row", "col"), check_vma=False)
```

```python
import jax
import jax.numpy as jnp
from jax import lax
from jax.experimental import pallas as pl
from jax.experimental.pallas import tpu as pltpu
from jax.sharding import PartitionSpec as P

MESH = pl.DeviceIdType.MESH
F32, BF16 = jnp.float32, jnp.bfloat16
B = 128
SWEEPS = 5
ROWS, COLS = 32, 8
RING = 8
PIECE = 32
WINDOWS = ((0, 0), (1, 0), (1, 1), (2, 0), (3, 0), (3, 1), (4, 0))
CHUNK = 256
CHUNKS = 1024 // CHUNK
COPIES = 130


def split(a):
    high = a.astype(BF16)
    return high, (a - high.astype(F32)).astype(BF16)


def split3(a):
    high = a.astype(BF16)
    rest = a - high.astype(F32)
    middle = rest.astype(BF16)
    return high, middle, (rest - middle.astype(F32)).astype(BF16)


def dot_terms(a, b, terms, dims):
    a = jnp.concatenate([a[i] for i, _ in terms], axis=dims[0][0])
    b = jnp.concatenate([b[j] for _, j in terms], axis=dims[1][0])
    return lax.dot_general(a, b, (dims, ((), ())), preferred_element_type=F32)


def dot3(a, b, dims=((1,), (0,))):
    return dot_terms(a, b, ((1, 0), (0, 1), (0, 0)), dims)


def dot6(a, b, dims=((1,), (0,))):
    return dot_terms(a, b, ((2, 0), (0, 2), (1, 1), (1, 0), (0, 1), (0, 0)), dims)


def gram_of(a):
    dims = (((0,), (0,)), ((), ()))
    return lax.dot_general(a, a, dims, precision=lax.Precision.HIGHEST, preferred_element_type=F32)


def inverses(grams, between):
    row = lax.broadcasted_iota(jnp.int32, (B, B), 0)
    col = lax.broadcasted_iota(jnp.int32, (B, B), 1)
    first = (col == row + 1) & ((row & 1) == 0)

    def start(gram):
        diagonal = jnp.where(row == col, gram, 0.0)
        down = 2.0 / jnp.sum(diagonal, axis=1, keepdims=True)
        along = 2.0 / jnp.sum(diagonal, axis=0, keepdims=True)
        return jnp.where(row == col, down, 0.0) - jnp.where(first, down * gram * along, 0.0)

    def narrow(inv, off):
        bands = [jnp.where((col - row == t) & ((col & (width - 1)) >= t), inv, 0.0) for t in range(width)]
        inner = sum((pltpu.roll(off, t, 1) if t else off) * jnp.sum(band, axis=0, keepdims=True) for t, band in enumerate(bands))
        return sum(
            jnp.sum(band, axis=1, keepdims=True) * (pltpu.roll(inner, B - t, 0) if t else inner) for t, band in enumerate(bands)
        )

    invs = [start(gram) for gram in grams]
    width = 2
    while width < B:
        pair = 2 * width
        corner = ((row & -pair) == (col & -pair)) & ((row & width) == 0) & ((col & width) != 0)
        offs = [jnp.where(corner, gram, 0.0) for gram in grams]
        if width < 8 and len(grams) == 1:
            invs = [inv - narrow(inv, off) for inv, off in zip(invs, offs)]
        elif width < 8:
            inner = [dot6(split3(inv), split3(off)) for inv, off in zip(invs, offs)]
            invs = [inv - dot6(split3(part), split3(inv)) for part, inv in zip(inner, invs)]
        else:
            parts = [inv.reshape(B // pair, pair, B) for inv in invs]
            uppers = [part[:, :width].reshape(B // 2, B) for part in parts]
            inner = [dot6(split3(upper), split3(off)) for upper, off in zip(uppers, offs)]
            uppers = [upper - dot6(split3(part), split3(inv)) for upper, part, inv in zip(uppers, inner, invs)]
            invs = [
                jnp.concatenate([upper.reshape(B // pair, width, B), part[:, width:]], axis=1).reshape(B, B)
                for upper, part in zip(uppers, parts)
            ]
        width = pair
        between.get(width, lambda: None)()
    return invs


def reflectors(panels, between):
    invs = inverses([gram_of(panel) for panel in panels], between)
    vs = [split(panel) for panel in panels]
    return [(v, dot6(split3(panel), split3(inv))) for v, panel, inv in zip(vs, panels, invs)]


def transform(reflector, top):
    v, vt = reflector
    rows = slice(0, B) if top else slice(B, 2 * B)
    row = lax.broadcasted_iota(jnp.int32, (B, 2 * B), 0) + (0 if top else B)
    col = lax.broadcasted_iota(jnp.int32, (B, 2 * B), 1)
    return split(jnp.where(row == col, 1.0, 0.0) - dot3(split(vt[rows]), v, ((1,), (1,))))


def kernel(
    z_hbm, panels_hbm, shift, slots, out_ref,
    z_in, panels, gathered0, gathered1, gathered2, gathered3, gathered4, near, far, along_x, pair, full,
    blocks, hh, hl, send_sem, recv_sem, own_sem,
):
    gathered = gathered0, gathered1, gathered2, gathered3, gathered4
    r, c = lax.axis_index("row"), lax.axis_index("col")
    k = lax.rem(r, 2)
    z = lax.rem(lax.div(r, 2), RING)
    h = lax.div(r, 2 * RING)
    row_of = lambda h_, z_, k_: (h_ * RING + z_) * 2 + k_
    ring = lambda d: lax.rem(z + d + RING, RING)
    ring_row = lambda d: row_of(h, ring(d), k)
    mate, across = row_of(h, z, 1 - k), row_of(1 - h, z, k)
    prev_row, next_row = lax.rem(r + ROWS - 1, ROWS), lax.rem(r + 1, ROWS)
    x, y = lax.div(c, 4), lax.rem(c, 4)
    in_line = lambda j: lax.rem(y + j + 4, 4)
    beside = lax.rem(c + 4, COLS)
    ids, sent = {}, []

    def remote(name, src, dst, row, col):
        i = ids.setdefault(name, len(ids))
        return pltpu.make_async_remote_copy(
            src_ref=src, dst_ref=dst, send_sem=send_sem.at[i], recv_sem=recv_sem.at[i],
            device_id=(row, col), device_id_type=MESH,
        )

    def send(name, src, dst, row, col):
        copy = remote(name, src, dst, row, col)
        copy.start()
        sent.append(copy)

    def arrive(name, dst):
        remote(name, dst, dst, mate, c).wait_recv()

    barrier = pltpu.get_barrier_semaphore()
    partners = [(ring_row(d), c) for d in range(1, RING)] + [(mate, c), (prev_row, c), (next_row, c)]
    partners += [(r, beside), (across, c), (across, beside)] + [(r, x * 4 + in_line(j)) for j in (1, 2, 3)]
    for partner in partners:
        pl.semaphore_signal(barrier, inc=1, device_id=partner, device_id_type=MESH)
    panels_copy = pltpu.make_async_copy(panels_hbm, panels, own_sem.at[0])
    panels_copy.start()
    z_copy = pltpu.make_async_copy(z_hbm, z_in, own_sem.at[1])
    z_copy.start()
    pl.semaphore_wait(barrier, len(partners))
    panels_copy.wait()

    def ring_send(s, distances):
        for d in distances:
            send(("ring", s, d), panels.at[s], gathered[s].at[k, z], ring_row(d), c)
        send(("mate", s, 0), panels.at[s], gathered[s].at[k, z], mate, c)

    def receive(s, distances):
        for d in distances:
            block = gathered[s].at[k, ring(-d)]
            arrive(("ring", s, d), block)
            send(("mate", s, d), block, block, mate, c)

    def pass_on(s):
        receive(s, (2, 6))
        for d, origin, target in ((3, -2, 1), (5, 2, -1), (4, 4 * k - 2, 2 - 4 * k)):
            block = gathered[s].at[k, ring(origin)]
            send(("ring", s, d), block, block, ring_row(target), c)
        receive(s, (1, 7))

    straight, nearest, rest = (4, 3, 5, 2, 6, 1, 7), (2, 6, 1, 7), (3, 5, 4)

    def receive_mate(s):
        for d in range(RING):
            arrive(("mate", s, d), gathered[s].at[1 - k, ring(-d)])

    ring_send(0, straight)
    ring_send(1, nearest)
    ring_send(2, nearest)
    for s in range(SWEEPS):
        gathered[s][k, z] = panels[s]

    def find(s, row):
        wanted = lax.rem(row + 2 * ROWS - shift[s], ROWS)
        slot = jnp.int32(0)
        for p in range(ROWS):
            slot = jnp.where(slots[s, p] == wanted, p, slot)
        return lax.div(slot, 2 * RING), (lax.rem(slot, 2), lax.rem(lax.div(slot, 2), RING))

    halves, places = zip(*[find(s, r - back) for s, back in WINDOWS])
    _, places_across = zip(*[find(s, across - back) for s, back in WINDOWS])
    def windows_of(*sweeps):
        ws = [w for w, (of, _) in enumerate(WINDOWS) if of in sweeps]
        return ws, pl.ds(ws[0], len(ws))

    def spread(*sweeps):
        ws, span = windows_of(*sweeps)
        for s in sweeps:
            receive_mate(s)
        for w in ws:
            s = WINDOWS[w][0]
            near[w] = gathered[s][places[w]]
            far[w] = gathered[s][places_across[w]]
        send(("far", sweeps), far.at[span], along_x.at[1, span], across, c)
        send(("far beside", sweeps), far.at[span], along_x.at[2, span], across, beside)
        send(("near", sweeps), near.at[span], along_x.at[0, span], r, beside)

    def share(*sweeps):
        ws, span = windows_of(*sweeps)
        for i, name in enumerate(("near", "far", "far beside")):
            arrive((name, sweeps), along_x.at[i, span])
        for w in ws:
            here = halves[w] == h
            for of_x, piece in (
                (x, jnp.where(here, near[w], along_x[1, w])),
                (1 - x, jnp.where(here, along_x[0, w], along_x[2, w])),
            ):
                pair[w, of_x] = piece
                full[w, of_x, y] = piece
        for j in (2, 1, 3):
            send(("share", sweeps, j), pair.at[span], full.at[span, :, y], r, x * 4 + in_line(j))

    def await_share(*sweeps):
        _, span = windows_of(*sweeps)
        for j in (1, 3, 2):
            arrive(("share", sweeps, j), full.at[span, :, in_line(-j)])

    receive(0, (1, 7, 2, 6))
    ring_send(3, nearest)
    ring_send(4, nearest)
    receive(0, rest)
    pass_on(1)
    spread(0)
    pass_on(2)
    receive(1, rest)
    pass_on(3)
    pass_on(4)
    spread(1)
    share(0)
    receive(2, rest)
    spread(2)
    share(1)
    receive(3, rest)
    receive(4, rest)
    await_share(0)

    def halfway():
        share(2)
        spread(3, 4)

    (first,) = reflectors([full[0].reshape(2 * B, B)], {16: halfway})
    hh[0, :B], hl[0, :B] = transform(first, True)
    hh[0, B:], hl[0, B:] = transform(first, False)
    z_copy.wait()

    def times(s, rows, block):
        return dot3((hh[s, rows], hl[s, rows]), block)

    low, high, both = slice(0, B), slice(B, 2 * B), slice(0, 2 * B)

    def exchange(x, j):
        mine = blocks.at[x, j]
        send(("prev", x, j), mine.at[pl.ds(B, B)], mine.at[pl.ds(3 * B, B)], prev_row, c)
        send(("next", x, j), mine.at[pl.ds(2 * B, B)], mine.at[pl.ds(0, B)], next_row, c)

    def odd_even(x, j):
        s = 2 * x + 1
        mine = blocks.at[x, j]
        arrive(("prev", x, j), mine.at[pl.ds(3 * B, B)])
        arrive(("next", x, j), mine.at[pl.ds(0, B)])
        new_low = times(s, low, split(mine[0 : 2 * B]))
        new_high = times(s, high, split(mine[2 * B : 4 * B]))
        return times(s + 1, both, split(jnp.concatenate([new_low, new_high], axis=0)))

    def transforms(ws, between={}):
        s = WINDOWS[ws[0]][0]
        own, back, even = reflectors([full[w].reshape(2 * B, B) for w in ws], between)
        hh[s, low], hl[s, low] = transform(back, False)
        hh[s, high], hl[s, high] = transform(own, True)
        hh[s + 1, low], hl[s + 1, low] = transform(even, True)
        hh[s + 1, high], hl[s + 1, high] = transform(even, False)

    for j in range(CHUNKS):
        cols = slice(j * CHUNK, (j + 1) * CHUNK)
        blocks[0, j, B : 3 * B] = times(0, both, split(z_in[:, cols]))
        exchange(0, j)
    await_share(1)
    share(3, 4)
    await_share(2)
    transforms((1, 2, 3))
    for j in range(CHUNKS):
        blocks[1, j, B : 3 * B] = odd_even(0, j)
        exchange(1, j)
    await_share(3, 4)
    transforms((4, 5, 6))
    for j in range(CHUNKS):
        out_ref[:, j * CHUNK : (j + 1) * CHUNK] = odd_even(1, j)
    for copy in sent:
        copy.wait_send()


def on_device(eigvecs, panels, sweep_shift, slot_group):
    rows, cols = eigvecs.shape
    hbm, smem = pl.BlockSpec(memory_space=pl.ANY), pl.BlockSpec(memory_space=pltpu.SMEM)
    return pl.pallas_call(
        kernel,
        out_shape=pltpu.VMEM((rows, cols), F32),
        in_specs=[hbm, hbm, smem, smem],
        out_specs=pl.BlockSpec(memory_space=pltpu.VMEM),
        scratch_shapes=[
            pltpu.VMEM((rows, cols), F32),
            pltpu.VMEM((SWEEPS, PIECE, B), F32),
            *[pltpu.VMEM((2, RING, PIECE, B), F32)] * SWEEPS,
            pltpu.VMEM((len(WINDOWS), PIECE, B), F32),
            pltpu.VMEM((len(WINDOWS), PIECE, B), F32),
            pltpu.VMEM((3, len(WINDOWS), PIECE, B), F32),
            pltpu.VMEM((len(WINDOWS), 2, PIECE, B), F32),
            pltpu.VMEM((len(WINDOWS), 2, 4, PIECE, B), F32),
            pltpu.VMEM((2, CHUNKS, 4 * B, CHUNK), F32),
            pltpu.VMEM((SWEEPS, 2 * B, 2 * B), BF16),
            pltpu.VMEM((SWEEPS, 2 * B, 2 * B), BF16),
            pltpu.SemaphoreType.DMA((COPIES,)),
            pltpu.SemaphoreType.DMA((COPIES,)),
            pltpu.SemaphoreType.DMA((2,)),
        ],
        compiler_params=pltpu.CompilerParams(collective_id=0, has_side_effects=True),
    )(eigvecs, panels.reshape(SWEEPS, PIECE, B), sweep_shift, slot_group)


def solution(mesh):
    in_specs = (P("row", "col"), P(None, "row", "col", None), P(), P())
    return jax.shard_map(on_device, mesh=mesh, in_specs=in_specs, out_specs=P("row", "col"), check_vma=False)
```

```python
import jax
import jax.numpy as jnp
from jax import lax
from jax.experimental import pallas as pl
from jax.experimental.pallas import tpu as pltpu
from jax.sharding import PartitionSpec as P

MESH = pl.DeviceIdType.MESH
F32, BF16 = jnp.float32, jnp.bfloat16
B = 128
SWEEPS = 5
ROWS, COLS = 32, 8
RING = 8
PIECE = 32
WINDOWS = ((0, 0), (1, 0), (1, 1), (2, 0), (3, 0), (3, 1), (4, 0))
CHUNK = 256
CHUNKS = 1024 // CHUNK
COPIES = 130


def split(a):
    high = a.astype(BF16)
    return high, (a - high.astype(F32)).astype(BF16)


def split3(a):
    high = a.astype(BF16)
    rest = a - high.astype(F32)
    middle = rest.astype(BF16)
    return high, middle, (rest - middle.astype(F32)).astype(BF16)


def dot_terms(a, b, terms, dims):
    a = jnp.concatenate([a[i] for i, _ in terms], axis=dims[0][0])
    b = jnp.concatenate([b[j] for _, j in terms], axis=dims[1][0])
    return lax.dot_general(a, b, (dims, ((), ())), preferred_element_type=F32)


def dot3(a, b, dims=((1,), (0,))):
    return dot_terms(a, b, ((1, 0), (0, 1), (0, 0)), dims)


def dot6(a, b, dims=((1,), (0,))):
    return dot_terms(a, b, ((2, 0), (0, 2), (1, 1), (1, 0), (0, 1), (0, 0)), dims)


def gram_of(a):
    dims = (((0,), (0,)), ((), ()))
    return lax.dot_general(a, a, dims, precision=lax.Precision.HIGHEST, preferred_element_type=F32)


def inverses(grams, between):
    row = lax.broadcasted_iota(jnp.int32, (B, B), 0)
    col = lax.broadcasted_iota(jnp.int32, (B, B), 1)
    first = (col == row + 1) & ((row & 1) == 0)

    def start(gram):
        diagonal = jnp.where(row == col, gram, 0.0)
        down = 2.0 / jnp.sum(diagonal, axis=1, keepdims=True)
        along = 2.0 / jnp.sum(diagonal, axis=0, keepdims=True)
        return jnp.where(row == col, down, 0.0) - jnp.where(first, down * gram * along, 0.0)

    def narrow(inv, off):
        bands = [jnp.where((col - row == t) & ((col & (width - 1)) >= t), inv, 0.0) for t in range(width)]
        inner = sum((pltpu.roll(off, t, 1) if t else off) * jnp.sum(band, axis=0, keepdims=True) for t, band in enumerate(bands))
        return sum(
            jnp.sum(band, axis=1, keepdims=True) * (pltpu.roll(inner, B - t, 0) if t else inner) for t, band in enumerate(bands)
        )

    invs = [start(gram) for gram in grams]
    width = 2
    while width < B:
        pair = 2 * width
        corner = ((row & -pair) == (col & -pair)) & ((row & width) == 0) & ((col & width) != 0)
        offs = [jnp.where(corner, gram, 0.0) for gram in grams]
        if width < 8 and len(grams) == 1:
            invs = [inv - narrow(inv, off) for inv, off in zip(invs, offs)]
        elif width < 8:
            inner = [dot6(split3(inv), split3(off)) for inv, off in zip(invs, offs)]
            invs = [inv - dot6(split3(part), split3(inv)) for part, inv in zip(inner, invs)]
        else:
            parts = [inv.reshape(B // pair, pair, B) for inv in invs]
            uppers = [part[:, :width].reshape(B // 2, B) for part in parts]
            inner = [dot6(split3(upper), split3(off)) for upper, off in zip(uppers, offs)]
            uppers = [upper - dot6(split3(part), split3(inv)) for upper, part, inv in zip(uppers, inner, invs)]
            invs = [
                jnp.concatenate([upper.reshape(B // pair, width, B), part[:, width:]], axis=1).reshape(B, B)
                for upper, part in zip(uppers, parts)
            ]
        width = pair
        between.get(width, lambda: None)()
    return invs


def reflectors(panels, between):
    invs = inverses([gram_of(panel) for panel in panels], between)
    vs = [split(panel) for panel in panels]
    return [(v, dot6(split3(panel), split3(inv))) for v, panel, inv in zip(vs, panels, invs)]


def transform(reflector, top):
    v, vt = reflector
    rows = slice(0, B) if top else slice(B, 2 * B)
    row = lax.broadcasted_iota(jnp.int32, (B, 2 * B), 0) + (0 if top else B)
    col = lax.broadcasted_iota(jnp.int32, (B, 2 * B), 1)
    return split(jnp.where(row == col, 1.0, 0.0) - dot3(split(vt[rows]), v, ((1,), (1,))))


def kernel(
    z_hbm, panels_hbm, shift, slots, out_ref,
    z_in, panels, gathered0, gathered1, gathered2, gathered3, gathered4, near, far, along_x, pair, full,
    blocks, hh, hl, send_sem, recv_sem, own_sem,
):
    gathered = gathered0, gathered1, gathered2, gathered3, gathered4
    r, c = lax.axis_index("row"), lax.axis_index("col")
    k = lax.rem(r, 2)
    z = lax.rem(lax.div(r, 2), RING)
    h = lax.div(r, 2 * RING)
    row_of = lambda h_, z_, k_: (h_ * RING + z_) * 2 + k_
    ring = lambda d: lax.rem(z + d + RING, RING)
    ring_row = lambda d: row_of(h, ring(d), k)
    mate, across = row_of(h, z, 1 - k), row_of(1 - h, z, k)
    prev_row, next_row = lax.rem(r + ROWS - 1, ROWS), lax.rem(r + 1, ROWS)
    x, y = lax.div(c, 4), lax.rem(c, 4)
    in_line = lambda j: lax.rem(y + j + 4, 4)
    beside = lax.rem(c + 4, COLS)
    ids, sent = {}, []

    def remote(name, src, dst, row, col):
        i = ids.setdefault(name, len(ids))
        return pltpu.make_async_remote_copy(
            src_ref=src, dst_ref=dst, send_sem=send_sem.at[i], recv_sem=recv_sem.at[i],
            device_id=(row, col), device_id_type=MESH,
        )

    def send(name, src, dst, row, col):
        copy = remote(name, src, dst, row, col)
        copy.start()
        sent.append(copy)

    def arrive(name, dst):
        remote(name, dst, dst, mate, c).wait_recv()

    barrier = pltpu.get_barrier_semaphore()
    partners = [(ring_row(d), c) for d in range(1, RING)] + [(mate, c), (prev_row, c), (next_row, c)]
    partners += [(r, beside), (across, c), (across, beside)] + [(r, x * 4 + in_line(j)) for j in (1, 2, 3)]
    for partner in partners:
        pl.semaphore_signal(barrier, inc=1, device_id=partner, device_id_type=MESH)
    panels_copy = pltpu.make_async_copy(panels_hbm, panels, own_sem.at[0])
    panels_copy.start()
    z_copy = pltpu.make_async_copy(z_hbm, z_in, own_sem.at[1])
    z_copy.start()
    pl.semaphore_wait(barrier, len(partners))
    panels_copy.wait()

    def ring_send(s, distances):
        for d in distances:
            send(("ring", s, d), panels.at[s], gathered[s].at[k, z], ring_row(d), c)
        send(("mate", s, 0), panels.at[s], gathered[s].at[k, z], mate, c)

    def receive(s, distances):
        for d in distances:
            block = gathered[s].at[k, ring(-d)]
            arrive(("ring", s, d), block)
            send(("mate", s, d), block, block, mate, c)

    def pass_on(s):
        receive(s, (2, 6))
        for d, origin, target in ((3, -2, 1), (5, 2, -1), (4, 4 * k - 2, 2 - 4 * k)):
            block = gathered[s].at[k, ring(origin)]
            send(("ring", s, d), block, block, ring_row(target), c)
        receive(s, (1, 7))

    straight, nearest, rest = (4, 3, 5, 2, 6, 1, 7), (2, 6, 1, 7), (3, 5, 4)

    def receive_mate(s):
        for d in range(RING):
            arrive(("mate", s, d), gathered[s].at[1 - k, ring(-d)])

    ring_send(0, straight)
    ring_send(1, nearest)
    ring_send(2, nearest)
    for s in range(SWEEPS):
        gathered[s][k, z] = panels[s]

    def find(s, row):
        wanted = lax.rem(row + 2 * ROWS - shift[s], ROWS)
        slot = jnp.int32(0)
        for p in range(ROWS):
            slot = jnp.where(slots[s, p] == wanted, p, slot)
        return lax.div(slot, 2 * RING), (lax.rem(slot, 2), lax.rem(lax.div(slot, 2), RING))

    halves, places = zip(*[find(s, r - back) for s, back in WINDOWS])
    _, places_across = zip(*[find(s, across - back) for s, back in WINDOWS])
    def windows_of(*sweeps):
        ws = [w for w, (of, _) in enumerate(WINDOWS) if of in sweeps]
        return ws, pl.ds(ws[0], len(ws))

    def spread(*sweeps):
        ws, span = windows_of(*sweeps)
        for s in sweeps:
            receive_mate(s)
        for w in ws:
            s = WINDOWS[w][0]
            near[w] = gathered[s][places[w]]
            far[w] = gathered[s][places_across[w]]
        send(("far", sweeps), far.at[span], along_x.at[1, span], across, c)
        send(("far beside", sweeps), far.at[span], along_x.at[2, span], across, beside)
        send(("near", sweeps), near.at[span], along_x.at[0, span], r, beside)

    def share(*sweeps):
        ws, span = windows_of(*sweeps)
        for i, name in enumerate(("near", "far", "far beside")):
            arrive((name, sweeps), along_x.at[i, span])
        for w in ws:
            here = halves[w] == h
            for of_x, piece in (
                (x, jnp.where(here, near[w], along_x[1, w])),
                (1 - x, jnp.where(here, along_x[0, w], along_x[2, w])),
            ):
                pair[w, of_x] = piece
                full[w, of_x, y] = piece
        for j in (2, 1, 3):
            send(("share", sweeps, j), pair.at[span], full.at[span, :, y], r, x * 4 + in_line(j))

    def await_share(*sweeps):
        _, span = windows_of(*sweeps)
        for j in (1, 3, 2):
            arrive(("share", sweeps, j), full.at[span, :, in_line(-j)])

    receive(0, (1, 7, 2, 6))
    ring_send(3, nearest)
    ring_send(4, nearest)
    receive(0, rest)
    pass_on(1)
    spread(0)
    pass_on(2)
    receive(1, rest)
    pass_on(3)
    pass_on(4)
    spread(1)
    share(0)
    receive(2, rest)
    spread(2)
    share(1)
    receive(3, rest)
    receive(4, rest)
    await_share(0)
    spread(3, 4)
    (first,) = reflectors([full[0].reshape(2 * B, B)], {16: lambda: share(2)})
    hh[0, :B], hl[0, :B] = transform(first, True)
    hh[0, B:], hl[0, B:] = transform(first, False)
    z_copy.wait()

    def times(s, rows, block):
        return dot3((hh[s, rows], hl[s, rows]), block)

    low, high, both = slice(0, B), slice(B, 2 * B), slice(0, 2 * B)

    def exchange(x, j):
        mine = blocks.at[x, j]
        send(("prev", x, j), mine.at[pl.ds(B, B)], mine.at[pl.ds(3 * B, B)], prev_row, c)
        send(("next", x, j), mine.at[pl.ds(2 * B, B)], mine.at[pl.ds(0, B)], next_row, c)

    def odd_even(x, j):
        s = 2 * x + 1
        mine = blocks.at[x, j]
        arrive(("prev", x, j), mine.at[pl.ds(3 * B, B)])
        arrive(("next", x, j), mine.at[pl.ds(0, B)])
        new_low = times(s, low, split(mine[0 : 2 * B]))
        new_high = times(s, high, split(mine[2 * B : 4 * B]))
        return times(s + 1, both, split(jnp.concatenate([new_low, new_high], axis=0)))

    def transforms(ws, between={}):
        s = WINDOWS[ws[0]][0]
        own, back, even = reflectors([full[w].reshape(2 * B, B) for w in ws], between)
        hh[s, low], hl[s, low] = transform(back, False)
        hh[s, high], hl[s, high] = transform(own, True)
        hh[s + 1, low], hl[s + 1, low] = transform(even, True)
        hh[s + 1, high], hl[s + 1, high] = transform(even, False)

    for j in range(CHUNKS):
        cols = slice(j * CHUNK, (j + 1) * CHUNK)
        blocks[0, j, B : 3 * B] = times(0, both, split(z_in[:, cols]))
        exchange(0, j)
    await_share(1)
    share(3, 4)
    await_share(2)
    transforms((1, 2, 3))
    for j in range(CHUNKS):
        blocks[1, j, B : 3 * B] = odd_even(0, j)
        exchange(1, j)
    await_share(3, 4)
    transforms((4, 5, 6))
    for j in range(CHUNKS):
        out_ref[:, j * CHUNK : (j + 1) * CHUNK] = odd_even(1, j)
    for copy in sent:
        copy.wait_send()


def on_device(eigvecs, panels, sweep_shift, slot_group):
    rows, cols = eigvecs.shape
    hbm, smem = pl.BlockSpec(memory_space=pl.ANY), pl.BlockSpec(memory_space=pltpu.SMEM)
    return pl.pallas_call(
        kernel,
        out_shape=pltpu.VMEM((rows, cols), F32),
        in_specs=[hbm, hbm, smem, smem],
        out_specs=pl.BlockSpec(memory_space=pltpu.VMEM),
        scratch_shapes=[
            pltpu.VMEM((rows, cols), F32),
            pltpu.VMEM((SWEEPS, PIECE, B), F32),
            *[pltpu.VMEM((2, RING, PIECE, B), F32)] * SWEEPS,
            pltpu.VMEM((len(WINDOWS), PIECE, B), F32),
            pltpu.VMEM((len(WINDOWS), PIECE, B), F32),
            pltpu.VMEM((3, len(WINDOWS), PIECE, B), F32),
            pltpu.VMEM((len(WINDOWS), 2, PIECE, B), F32),
            pltpu.VMEM((len(WINDOWS), 2, 4, PIECE, B), F32),
            pltpu.VMEM((2, CHUNKS, 4 * B, CHUNK), F32),
            pltpu.VMEM((SWEEPS, 2 * B, 2 * B), BF16),
            pltpu.VMEM((SWEEPS, 2 * B, 2 * B), BF16),
            pltpu.SemaphoreType.DMA((COPIES,)),
            pltpu.SemaphoreType.DMA((COPIES,)),
            pltpu.SemaphoreType.DMA((2,)),
        ],
        compiler_params=pltpu.CompilerParams(collective_id=0, has_side_effects=True),
    )(eigvecs, panels.reshape(SWEEPS, PIECE, B), sweep_shift, slot_group)


def solution(mesh):
    in_specs = (P("row", "col"), P(None, "row", "col", None), P(), P())
    return jax.shard_map(on_device, mesh=mesh, in_specs=in_specs, out_specs=P("row", "col"), check_vma=False)
```

```python
import jax
import jax.numpy as jnp
from jax import lax
from jax.experimental import pallas as pl
from jax.experimental.pallas import tpu as pltpu
from jax.sharding import PartitionSpec as P

MESH = pl.DeviceIdType.MESH
F32, BF16 = jnp.float32, jnp.bfloat16
B = 128
SWEEPS = 5
ROWS, COLS = 32, 8
RING = 8
PIECE = 32
WINDOWS = ((0, 0), (1, 0), (1, 1), (2, 0), (3, 0), (3, 1), (4, 0))
CHUNK = 256
CHUNKS = 1024 // CHUNK
COPIES = 130


def split(a):
    high = a.astype(BF16)
    return high, (a - high.astype(F32)).astype(BF16)


def split3(a):
    high = a.astype(BF16)
    rest = a - high.astype(F32)
    middle = rest.astype(BF16)
    return high, middle, (rest - middle.astype(F32)).astype(BF16)


def dot_terms(a, b, terms, dims):
    a = jnp.concatenate([a[i] for i, _ in terms], axis=dims[0][0])
    b = jnp.concatenate([b[j] for _, j in terms], axis=dims[1][0])
    return lax.dot_general(a, b, (dims, ((), ())), preferred_element_type=F32)


def dot3(a, b, dims=((1,), (0,))):
    return dot_terms(a, b, ((1, 0), (0, 1), (0, 0)), dims)


def dot6(a, b, dims=((1,), (0,))):
    return dot_terms(a, b, ((2, 0), (0, 2), (1, 1), (1, 0), (0, 1), (0, 0)), dims)


def gram_of(a):
    dims = (((0,), (0,)), ((), ()))
    return lax.dot_general(a, a, dims, precision=lax.Precision.HIGHEST, preferred_element_type=F32)


def inverses(grams, between):
    row = lax.broadcasted_iota(jnp.int32, (B, B), 0)
    col = lax.broadcasted_iota(jnp.int32, (B, B), 1)
    first = (col == row + 1) & ((row & 1) == 0)

    def start(gram):
        diagonal = jnp.where(row == col, gram, 0.0)
        down = 2.0 / jnp.sum(diagonal, axis=1, keepdims=True)
        along = 2.0 / jnp.sum(diagonal, axis=0, keepdims=True)
        return jnp.where(row == col, down, 0.0) - jnp.where(first, down * gram * along, 0.0)

    def narrow(inv, off):
        bands = [jnp.where((col - row == t) & ((col & (width - 1)) >= t), inv, 0.0) for t in range(width)]
        inner = sum((pltpu.roll(off, t, 1) if t else off) * jnp.sum(band, axis=0, keepdims=True) for t, band in enumerate(bands))
        return sum(
            jnp.sum(band, axis=1, keepdims=True) * (pltpu.roll(inner, B - t, 0) if t else inner) for t, band in enumerate(bands)
        )

    invs = [start(gram) for gram in grams]
    width = 2
    while width < B:
        pair = 2 * width
        corner = ((row & -pair) == (col & -pair)) & ((row & width) == 0) & ((col & width) != 0)
        offs = [jnp.where(corner, gram, 0.0) for gram in grams]
        if width == 2 or width < 8 and len(grams) == 1:
            invs = [inv - narrow(inv, off) for inv, off in zip(invs, offs)]
        elif width < 8:
            inner = [dot6(split3(inv), split3(off)) for inv, off in zip(invs, offs)]
            invs = [inv - dot6(split3(part), split3(inv)) for part, inv in zip(inner, invs)]
        else:
            parts = [inv.reshape(B // pair, pair, B) for inv in invs]
            uppers = [part[:, :width].reshape(B // 2, B) for part in parts]
            inner = [dot6(split3(upper), split3(off)) for upper, off in zip(uppers, offs)]
            uppers = [upper - dot6(split3(part), split3(inv)) for upper, part, inv in zip(uppers, inner, invs)]
            invs = [
                jnp.concatenate([upper.reshape(B // pair, width, B), part[:, width:]], axis=1).reshape(B, B)
                for upper, part in zip(uppers, parts)
            ]
        width = pair
        between.get(width, lambda: None)()
    return invs


def reflectors(panels, between):
    invs = inverses([gram_of(panel) for panel in panels], between)
    vs = [split(panel) for panel in panels]
    return [(v, dot6(split3(panel), split3(inv))) for v, panel, inv in zip(vs, panels, invs)]


def transform(reflector, top):
    v, vt = reflector
    rows = slice(0, B) if top else slice(B, 2 * B)
    row = lax.broadcasted_iota(jnp.int32, (B, 2 * B), 0) + (0 if top else B)
    col = lax.broadcasted_iota(jnp.int32, (B, 2 * B), 1)
    return split(jnp.where(row == col, 1.0, 0.0) - dot3(split(vt[rows]), v, ((1,), (1,))))


def kernel(
    z_hbm, panels_hbm, shift, slots, out_ref,
    z_in, panels, gathered0, gathered1, gathered2, gathered3, gathered4, near, far, along_x, pair, full,
    blocks, hh, hl, send_sem, recv_sem, own_sem,
):
    gathered = gathered0, gathered1, gathered2, gathered3, gathered4
    r, c = lax.axis_index("row"), lax.axis_index("col")
    k = lax.rem(r, 2)
    z = lax.rem(lax.div(r, 2), RING)
    h = lax.div(r, 2 * RING)
    row_of = lambda h_, z_, k_: (h_ * RING + z_) * 2 + k_
    ring = lambda d: lax.rem(z + d + RING, RING)
    ring_row = lambda d: row_of(h, ring(d), k)
    mate, across = row_of(h, z, 1 - k), row_of(1 - h, z, k)
    prev_row, next_row = lax.rem(r + ROWS - 1, ROWS), lax.rem(r + 1, ROWS)
    x, y = lax.div(c, 4), lax.rem(c, 4)
    in_line = lambda j: lax.rem(y + j + 4, 4)
    beside = lax.rem(c + 4, COLS)
    ids, sent = {}, []

    def remote(name, src, dst, row, col):
        i = ids.setdefault(name, len(ids))
        return pltpu.make_async_remote_copy(
            src_ref=src, dst_ref=dst, send_sem=send_sem.at[i], recv_sem=recv_sem.at[i],
            device_id=(row, col), device_id_type=MESH,
        )

    def send(name, src, dst, row, col):
        copy = remote(name, src, dst, row, col)
        copy.start()
        sent.append(copy)

    def arrive(name, dst):
        remote(name, dst, dst, mate, c).wait_recv()

    barrier = pltpu.get_barrier_semaphore()
    partners = [(ring_row(d), c) for d in range(1, RING)] + [(mate, c), (prev_row, c), (next_row, c)]
    partners += [(r, beside), (across, c), (across, beside)] + [(r, x * 4 + in_line(j)) for j in (1, 2, 3)]
    for partner in partners:
        pl.semaphore_signal(barrier, inc=1, device_id=partner, device_id_type=MESH)
    panels_copy = pltpu.make_async_copy(panels_hbm, panels, own_sem.at[0])
    panels_copy.start()
    z_copy = pltpu.make_async_copy(z_hbm, z_in, own_sem.at[1])
    z_copy.start()
    pl.semaphore_wait(barrier, len(partners))
    panels_copy.wait()

    def ring_send(s, distances):
        for d in distances:
            send(("ring", s, d), panels.at[s], gathered[s].at[k, z], ring_row(d), c)
        send(("mate", s, 0), panels.at[s], gathered[s].at[k, z], mate, c)

    def receive(s, distances):
        for d in distances:
            block = gathered[s].at[k, ring(-d)]
            arrive(("ring", s, d), block)
            send(("mate", s, d), block, block, mate, c)

    def pass_on(s):
        receive(s, (2, 6))
        for d, origin, target in ((3, -2, 1), (5, 2, -1), (4, 4 * k - 2, 2 - 4 * k)):
            block = gathered[s].at[k, ring(origin)]
            send(("ring", s, d), block, block, ring_row(target), c)
        receive(s, (1, 7))

    straight, nearest, rest = (4, 3, 5, 2, 6, 1, 7), (2, 6, 1, 7), (3, 5, 4)

    def receive_mate(s):
        for d in range(RING):
            arrive(("mate", s, d), gathered[s].at[1 - k, ring(-d)])

    ring_send(0, straight)
    ring_send(1, nearest)
    ring_send(2, nearest)
    for s in range(SWEEPS):
        gathered[s][k, z] = panels[s]

    def find(s, row):
        wanted = lax.rem(row + 2 * ROWS - shift[s], ROWS)
        slot = jnp.int32(0)
        for p in range(ROWS):
            slot = jnp.where(slots[s, p] == wanted, p, slot)
        return lax.div(slot, 2 * RING), (lax.rem(slot, 2), lax.rem(lax.div(slot, 2), RING))

    halves, places = zip(*[find(s, r - back) for s, back in WINDOWS])
    _, places_across = zip(*[find(s, across - back) for s, back in WINDOWS])
    def windows_of(*sweeps):
        ws = [w for w, (of, _) in enumerate(WINDOWS) if of in sweeps]
        return ws, pl.ds(ws[0], len(ws))

    def spread(*sweeps):
        ws, span = windows_of(*sweeps)
        for s in sweeps:
            receive_mate(s)
        for w in ws:
            s = WINDOWS[w][0]
            near[w] = gathered[s][places[w]]
            far[w] = gathered[s][places_across[w]]
        send(("far", sweeps), far.at[span], along_x.at[1, span], across, c)
        send(("far beside", sweeps), far.at[span], along_x.at[2, span], across, beside)
        send(("near", sweeps), near.at[span], along_x.at[0, span], r, beside)

    def share(*sweeps):
        ws, span = windows_of(*sweeps)
        for i, name in enumerate(("near", "far", "far beside")):
            arrive((name, sweeps), along_x.at[i, span])
        for w in ws:
            here = halves[w] == h
            for of_x, piece in (
                (x, jnp.where(here, near[w], along_x[1, w])),
                (1 - x, jnp.where(here, along_x[0, w], along_x[2, w])),
            ):
                pair[w, of_x] = piece
                full[w, of_x, y] = piece
        for j in (2, 1, 3):
            send(("share", sweeps, j), pair.at[span], full.at[span, :, y], r, x * 4 + in_line(j))

    def await_share(*sweeps):
        _, span = windows_of(*sweeps)
        for j in (1, 3, 2):
            arrive(("share", sweeps, j), full.at[span, :, in_line(-j)])

    receive(0, (1, 7, 2, 6))
    ring_send(3, nearest)
    ring_send(4, nearest)
    receive(0, rest)
    pass_on(1)
    spread(0)
    pass_on(2)
    receive(1, rest)
    pass_on(3)
    pass_on(4)
    spread(1)
    share(0)
    receive(2, rest)
    spread(2)
    share(1)
    receive(3, rest)
    receive(4, rest)
    await_share(0)
    spread(3, 4)
    (first,) = reflectors([full[0].reshape(2 * B, B)], {16: lambda: share(2)})
    hh[0, :B], hl[0, :B] = transform(first, True)
    hh[0, B:], hl[0, B:] = transform(first, False)
    z_copy.wait()

    def times(s, rows, block):
        return dot3((hh[s, rows], hl[s, rows]), block)

    low, high, both = slice(0, B), slice(B, 2 * B), slice(0, 2 * B)

    def exchange(x, j):
        mine = blocks.at[x, j]
        send(("prev", x, j), mine.at[pl.ds(B, B)], mine.at[pl.ds(3 * B, B)], prev_row, c)
        send(("next", x, j), mine.at[pl.ds(2 * B, B)], mine.at[pl.ds(0, B)], next_row, c)

    def odd_even(x, j):
        s = 2 * x + 1
        mine = blocks.at[x, j]
        arrive(("prev", x, j), mine.at[pl.ds(3 * B, B)])
        arrive(("next", x, j), mine.at[pl.ds(0, B)])
        new_low = times(s, low, split(mine[0 : 2 * B]))
        new_high = times(s, high, split(mine[2 * B : 4 * B]))
        return times(s + 1, both, split(jnp.concatenate([new_low, new_high], axis=0)))

    def transforms(ws, between={}):
        s = WINDOWS[ws[0]][0]
        own, back, even = reflectors([full[w].reshape(2 * B, B) for w in ws], between)
        hh[s, low], hl[s, low] = transform(back, False)
        hh[s, high], hl[s, high] = transform(own, True)
        hh[s + 1, low], hl[s + 1, low] = transform(even, True)
        hh[s + 1, high], hl[s + 1, high] = transform(even, False)

    for j in range(CHUNKS):
        cols = slice(j * CHUNK, (j + 1) * CHUNK)
        blocks[0, j, B : 3 * B] = times(0, both, split(z_in[:, cols]))
        exchange(0, j)
    await_share(1)
    share(3, 4)
    await_share(2)
    transforms((1, 2, 3))
    for j in range(CHUNKS):
        blocks[1, j, B : 3 * B] = odd_even(0, j)
        exchange(1, j)
    await_share(3, 4)
    transforms((4, 5, 6))
    for j in range(CHUNKS):
        out_ref[:, j * CHUNK : (j + 1) * CHUNK] = odd_even(1, j)
    for copy in sent:
        copy.wait_send()


def on_device(eigvecs, panels, sweep_shift, slot_group):
    rows, cols = eigvecs.shape
    hbm, smem = pl.BlockSpec(memory_space=pl.ANY), pl.BlockSpec(memory_space=pltpu.SMEM)
    return pl.pallas_call(
        kernel,
        out_shape=pltpu.VMEM((rows, cols), F32),
        in_specs=[hbm, hbm, smem, smem],
        out_specs=pl.BlockSpec(memory_space=pltpu.VMEM),
        scratch_shapes=[
            pltpu.VMEM((rows, cols), F32),
            pltpu.VMEM((SWEEPS, PIECE, B), F32),
            *[pltpu.VMEM((2, RING, PIECE, B), F32)] * SWEEPS,
            pltpu.VMEM((len(WINDOWS), PIECE, B), F32),
            pltpu.VMEM((len(WINDOWS), PIECE, B), F32),
            pltpu.VMEM((3, len(WINDOWS), PIECE, B), F32),
            pltpu.VMEM((len(WINDOWS), 2, PIECE, B), F32),
            pltpu.VMEM((len(WINDOWS), 2, 4, PIECE, B), F32),
            pltpu.VMEM((2, CHUNKS, 4 * B, CHUNK), F32),
            pltpu.VMEM((SWEEPS, 2 * B, 2 * B), BF16),
            pltpu.VMEM((SWEEPS, 2 * B, 2 * B), BF16),
            pltpu.SemaphoreType.DMA((COPIES,)),
            pltpu.SemaphoreType.DMA((COPIES,)),
            pltpu.SemaphoreType.DMA((2,)),
        ],
        compiler_params=pltpu.CompilerParams(collective_id=0, has_side_effects=True),
    )(eigvecs, panels.reshape(SWEEPS, PIECE, B), sweep_shift, slot_group)


def solution(mesh):
    in_specs = (P("row", "col"), P(None, "row", "col", None), P(), P())
    return jax.shard_map(on_device, mesh=mesh, in_specs=in_specs, out_specs=P("row", "col"), check_vma=False)
```
